512 devices in a mesh: sec: 32 (over z_lo, x, core), tile: 16 (over y, z_hi).
Axes of the slice: x: 4, y: 4, z: 16 (z_hi: 4, z_lo: 4; z = z_hi * 4 + z_lo), core: 2. Of those that a mesh axis runs over, the one named last changes fastest.
Arguments:
- in_plane_force: float32 [2, 64, 1024, 256], P(None, 'sec', 'tile'), may hold values from -6 to 6
- stiffness: float32 [64, 1024, 256], P('sec', 'tile'), may hold values from 0.5 to 2
- stiffness_z: float32 [64, 1024, 256], P(None, ('tile', 'sec')), may hold values from 0.3 to 1.5
- patch_dest: int32 [32, 16, 256, 1], P('sec', 'tile'), may hold values from 0 to 31; in each aligned block of 256 rows (0 to 255, 256 to 511, ..., all dimensions but the last counted through in order) at most 16 rows name the same one
- patch_pos: int32 [32, 16, 256], P('sec', 'tile'), may hold values from 0 to 7
- patch_flow: float32 [32, 16, 256, 2, 128], P('sec', 'tile'), may hold values from -6 to 6
- patch_conf: float32 [32, 16, 256, 128], P('sec', 'tile'), may hold values from 0.2 to 1
Outputs:
- displacement: float32 [2, 64, 1024, 256], P(None, None, ('tile', 'sec'))
The draws below stay inside these ranges and needn't reach their ends.
Inputs may be any that keep to these rules, and one draw needn't show every extreme that they name: `patch_dest`: among the 256 patches of one section group and tile, at most 16 name the same owner; in some of them an owner is named exactly 16 times.
All inputs are finite; a program needn't handle non-finite values.
Results may differ from the reference program's by a relative error of at most 0.00002.
Values sent between devices are 32-bit elements; how exact they have to be, the bound alone decides.
A program may use at most 64 MiB of HBM per device.

```python
import math
import jax
import jax.numpy as jnp
import numpy as np
from jax import lax

ZD = 2
YD = 64
XN = 256
PW = 128
P_DEV = 256
ISTEPS = 8
ZSTEPS = 8
Z = 64
YT = 1024
YO = 2
XB = 2
CAP = 16
N_SEC = 32
N_TILE = 16


def touch_ends(entries, own_key, least, top_value):
    index_at = [jax.random.randint(jax.random.fold_in(own_key, axis), (), 0, length) for axis, length in enumerate(entries.shape)]
    longest = entries.shape.index(max(entries.shape))
    next_to = index_at[:longest] + [(index_at[longest] + 1) % entries.shape[longest]] + index_at[longest + 1:]
    return entries.at[tuple(index_at)].set(least).at[tuple(next_to)].set(top_value)


def shard_levels(stream_key, extent, shards, low, high):
    def one(axis_at, parts):
        heights = jax.random.uniform(jax.random.fold_in(jax.random.fold_in(stream_key, 6), axis_at), (parts,), jnp.float32, low / len(shards), high / len(shards))
        return jnp.repeat(jnp.exp(heights), extent[axis_at] // parts).reshape((-1,) + (1,) * (len(extent) - axis_at - 1))

    level = one(*shards[0])
    for cut in shards[1:]:
        level = level * one(*cut)
    return level


def shared_out(own_key, own, number, rows, count, top, limit, slope):
    order = jax.random.permutation(own_key, count)
    packed, common = load_shares(count, rows * top, limit, slope, True), load_shares(count, rows * top, limit, slope, False)
    places = jnp.arange(count)

    def named(sizes, turn):
        used = int((sizes > 0).sum())
        fixed = max(1, used // 4)
        passed = fixed + (places - fixed + turn * (used - fixed)) % max(1, count - fixed)
        return jnp.zeros((count,), jnp.int32).at[order[jnp.where(places < fixed, places, passed)]].set(jnp.asarray(sizes, jnp.int32))

    sizes = jnp.where(number % 4 == 0, named(packed, number // 4), named(common, number - number // 4 - 1))
    mixed = jax.random.permutation(jax.random.fold_in(own, 3), count)
    source_of, receiver = mixed[0:count // 2 * 2:2], mixed[1:count // 2 * 2:2]
    room = jnp.minimum(sizes[source_of] - 1, limit - sizes[receiver]) // 2
    room = jnp.where((source_of == order[0]) | (receiver == order[0]) | (sizes[receiver] == 0), 0, jnp.maximum(room, 0))
    passed = jax.random.randint(jax.random.fold_in(own, 4), (count // 2,), 0, 1 << 20) % (room + 1)
    sizes = sizes.at[source_of].add(-passed).at[receiver].add(passed)
    labels = jnp.searchsorted(jnp.cumsum(sizes), jnp.arange(rows * top), side="right").astype(jnp.int32)
    listing = labels.reshape(top, rows).T
    listing = listing[jax.random.permutation(jax.random.fold_in(own, 1), rows)]
    turn = jax.random.randint(jax.random.fold_in(own, 2), (rows, 1), 0, top)
    return jnp.take_along_axis(listing, (jnp.arange(top)[None, :] + turn) % top, axis=1)


def load_shares(count, total, most, lean, full):
    weights = [(1 << 20) // math.isqrt(rank ** lean) + 1 for rank in range(1, count + 1)]
    largest = most if full else min(most, max(-(-total // count), total * weights[0] // sum(weights)))
    least = 1 if total - largest >= count - 1 else 0
    counts, surplus = [largest] + [least] * (count - 1), total - largest - least * (count - 1)
    while surplus > 0:
        candidates = [i for i in range(1, count) if counts[i] < largest] or [i for i in range(1, count) if counts[i] < most]
        mass, remaining = sum([weights[i] for i in candidates]), surplus
        for i in candidates:
            extra = min(most - counts[i], max(1, remaining * weights[i] // mass), surplus)
            counts[i] = counts[i] + extra
            surplus = surplus - extra
    return np.array(counts)


def normal_values(rng, extent, width, bound, cuts=(), held_as=jnp.bfloat16):
    gain = shard_levels(rng, extent, cuts, -0.22, 0.18) if cuts else 1.0
    values = jax.random.normal(rng, extent, jnp.float32) * width * gain
    return jnp.minimum(jnp.maximum(values, -bound), bound).astype(held_as)


def setup_inputs(seed: int = 0) -> dict:
    keys = jax.random.split(jax.random.key(seed), 8)
    in_plane_force = normal_values(keys[0], (2, Z, YT, XN), 1.0, 6.0, ((1, 32), (2, 16)), jnp.float32)
    stiffness = jnp.clip(jnp.exp(math.log(2.0) - 1.3862944 * jax.random.uniform(keys[1], (Z, YT, XN), jnp.float32) ** shard_levels(keys[1], (Z, YT, XN), ((0, 32), (1, 16)), -0.2, 0.2)), 0.5, 2.0)
    stiffness_z = jnp.clip(jnp.exp(math.log(1.5) - 1.60943787 * jax.random.uniform(keys[2], (Z, YT, XN), jnp.float32) ** shard_levels(keys[2], (Z, YT, XN), ((1, 512),), -0.2, 0.2)), 0.3, 1.5)
    patch_dest_keys = jax.random.split(jax.random.fold_in(keys[3], 1), N_SEC * N_TILE * P_DEV // P_DEV)
    patch_dest_turns = jax.random.permutation(jax.random.fold_in(keys[3], 3), N_SEC * N_TILE * P_DEV // P_DEV)
    patch_dest = jax.vmap(lambda own, number: shared_out(jax.random.fold_in(keys[3], 2), own, number, P_DEV, N_SEC, 1, CAP, 2))(patch_dest_keys, patch_dest_turns).reshape((N_SEC, N_TILE, P_DEV, 1))
    patch_pos = touch_ends(jax.random.randint(keys[4], (N_SEC, N_TILE, P_DEV), 0, ZD * YO * XB), jax.random.fold_in(keys[4], 1), 0, (ZD * YO * XB) - 1).astype(jnp.int32)
    patch_flow = normal_values(keys[5], (N_SEC, N_TILE, P_DEV, 2, PW), 1.0, 6.0, ((0, 32), (1, 16)), jnp.float32)
    patch_conf = jnp.clip(0.2 + 0.8 * jax.random.uniform(keys[6], (N_SEC, N_TILE, P_DEV, PW), jnp.float32) ** shard_levels(keys[6], (N_SEC, N_TILE, P_DEV, PW), ((0, 32), (1, 16)), -0.2, 0.2), 0.2, 1.0)
    return {"in_plane_force": in_plane_force, "stiffness": stiffness, "stiffness_z": stiffness_z, "patch_dest": patch_dest, "patch_pos": patch_pos, "patch_flow": patch_flow, "patch_conf": patch_conf}


STEP_PLANE = 0.12
STEP_CROSS = 0.15


def plane_laplace(field):
    padded = jnp.pad(field, ((0, 0), (0, 0), (1, 1), (1, 1)))
    return padded[:, :, 2:, 1:-1] + padded[:, :, :-2, 1:-1] + padded[:, :, 1:-1, 2:] + padded[:, :, 1:-1, :-2] - 4.0 * field


def cross_steps(field, pull, weight, stiffness_z):
    for step in range(ZSTEPS):
        zero_layer = jnp.zeros(field.shape[:1] + (1,) + field.shape[2:], jnp.float32)
        below = jnp.concatenate([zero_layer, field[:, :-1]], axis=1)
        above = jnp.concatenate([field[:, 1:], zero_layer], axis=1)
        stretch = pull - weight[None] * (field - below)
        stretch_above = jnp.concatenate([stretch[:, 1:], zero_layer], axis=1)
        field = field + STEP_CROSS * (stiffness_z[None] * (above + below - 2.0 * field) + stretch - stretch_above)
    return field


def reference(in_plane_force, stiffness, stiffness_z, patch_dest, patch_pos, patch_flow, patch_conf):
    field = jnp.zeros(in_plane_force.shape, jnp.float32)
    for step in range(ISTEPS):
        field = field + STEP_PLANE * (stiffness[None] * plane_laplace(field) + in_plane_force)
    group = lax.broadcasted_iota(jnp.int32, (N_SEC, N_TILE, P_DEV), 0)
    tile_index = lax.broadcasted_iota(jnp.int32, (N_SEC, N_TILE, P_DEV), 1)
    layer = patch_pos // (YO * XB)
    inner_row = (patch_pos // XB) % YO
    column_block = patch_pos % XB
    section = group * ZD + layer
    node_row = tile_index * YD + patch_dest[..., 0] * YO + inner_row
    target = ((section * YT + node_row) * XB + column_block).reshape(-1).astype(jnp.int32)
    weighted = patch_conf[:, :, :, None, :] * patch_flow
    payload = jnp.concatenate([weighted, patch_conf[:, :, :, None, :]], axis=3).reshape(-1, 3, PW)
    grid = jnp.zeros((Z * YT * XB, 3, PW), jnp.float32).at[target].add(payload)
    grid = grid.reshape(Z, YT, XB, 3, PW).transpose(3, 0, 1, 2, 4).reshape(3, Z, YT, XN)
    return cross_steps(field, grid[:2], grid[2], stiffness_z)
```

```python
import functools

import jax
import jax.numpy as jnp
from jax import lax
from jax.experimental import pallas as pl
from jax.experimental.pallas import tpu as pltpu
from jax.sharding import PartitionSpec as P

ISTEPS = 8
ZSTEPS = 8
STEP_PLANE = 0.12
STEP_CROSS = 0.15
LANES = 128
HALO = 8


def plane_steps(force, stiff):
    column = lax.broadcasted_iota(jnp.int32, force.shape, 2)
    first, last = column == 0, column == force.shape[2] - 1
    field = STEP_PLANE * force
    for _ in range(1, ISTEPS):
        up = pltpu.roll(field, 1, 1)
        down = pltpu.roll(field, field.shape[1] - 1, 1)
        left = jnp.where(first, 0.0, pltpu.roll(field, 1, 2))
        right = jnp.where(last, 0.0, pltpu.roll(field, field.shape[2] - 1, 2))
        laplace = (up + down) + (left + right) - 4.0 * field
        field = field + STEP_PLANE * (stiff * laplace + force)
    return field


def split3(value):
    high = value.astype(jnp.bfloat16)
    rest = value - high.astype(jnp.float32)
    middle = rest.astype(jnp.bfloat16)
    low = (rest - middle.astype(jnp.float32)).astype(jnp.bfloat16)
    return high, middle, low


def pair_halves(a, b):
    lower = lax.broadcasted_iota(jnp.int32, a.shape, 1) < 4
    return jnp.where(lower, a, pltpu.roll(b, 4, 1)), jnp.where(lower, pltpu.roll(a, 4, 1), b)


def body(
    force_hbm, stiff_hbm, cross_hbm, dest_hbm, pos_hbm, flow_hbm, conf_hbm, out_ref,
    fbuf, sbuf, zbuf, dest, pos, flow, conf, vbuf,
    send_p, send_f, recv_f, recv_p, recv_w, other, wide_w, wide_k,
    local_sem, halo_send, halo_recv, p_send, p_recv, w_send, w_recv, f_send, f_recv,
):
    groups = lax.axis_size("sec")
    tiles = lax.axis_size("tile")
    me = lax.axis_index("sec")
    tile = lax.axis_index("tile")
    rows = force_hbm.shape[2]
    layers = force_hbm.shape[1]
    depth = groups * layers
    above, below = lax.rem(tile + 1, tiles), lax.rem(tile + tiles - 1, tiles)

    barrier = pltpu.get_barrier_semaphore()

    @pl.loop(1, groups)
    def _(k):
        pl.semaphore_signal(
            barrier, inc=1, device_id={"sec": lax.rem(me + k, groups)}, device_id_type=pl.DeviceIdType.MESH
        )

    for neighbour in (above, below):
        pl.semaphore_signal(barrier, inc=1, device_id={"tile": neighbour}, device_id_type=pl.DeviceIdType.MESH)

    loads = [
        pltpu.make_async_copy(source, target, local_sem.at[i])
        for i, (source, target) in enumerate(
            (
                (dest_hbm, dest),
                (pos_hbm, pos),
                (conf_hbm, conf),
                (flow_hbm, flow),
                (stiff_hbm, sbuf.at[:, pl.ds(HALO, rows), :]),
                (force_hbm, fbuf.at[:, :, pl.ds(HALO, rows), :]),
                (cross_hbm, zbuf),
            )
        )
    ]
    for load in loads:
        load.start()
    for load in loads[:4]:
        load.wait()

    count = conf.shape[0]
    place = pos[...]
    slot = dest[...] * 8 + (place // 4) * 4 + (place % 2) * 2 + (place // 2) % 2
    hot = (lax.broadcasted_iota(jnp.int32, (count, count), 0) == slot).astype(jnp.float32).astype(jnp.bfloat16)
    confidence = conf[...]
    payload = jnp.concatenate(
        [confidence * flow[pl.ds(0, count, stride=2), :], confidence * flow[pl.ds(1, count, stride=2), :], confidence],
        axis=1,
    )
    high, middle, low = [jnp.dot(hot, part, preferred_element_type=jnp.float32) for part in split3(payload)]
    grid = high + middle + low
    pull = [grid[:, c * LANES : (c + 1) * LANES].reshape(groups, 8, LANES) for c in range(2)]
    front, back = pair_halves(*pull)
    send_p[:, 0] = front
    send_p[:, 1] = back
    send_p[:, 2] = grid[:, 2 * LANES :].reshape(groups, 8, LANES)

    recv_f[0] = jnp.zeros_like(recv_f[0])
    recv_f[depth + 1] = jnp.zeros_like(recv_f[0])
    other[0] = jnp.zeros_like(recv_f[0])
    other[depth + 1] = jnp.zeros_like(recv_f[0])
    recv_p[depth] = jnp.zeros_like(recv_f[0])
    wide_w[depth] = jnp.zeros_like(recv_f[0])

    loads[4].wait()
    loads[5].wait()
    pl.semaphore_wait(barrier, groups - 1 + 2)

    def halo_copy(index, buffer, source, target, neighbour):
        lead = (slice(None),) * (len(buffer.shape) - 2)
        return pltpu.make_async_remote_copy(
            src_ref=buffer.at[lead + (pl.ds(source, HALO), slice(None))],
            dst_ref=buffer.at[lead + (pl.ds(target, HALO), slice(None))],
            send_sem=halo_send.at[index],
            recv_sem=halo_recv.at[index],
            device_id={"tile": neighbour},
            device_id_type=pl.DeviceIdType.MESH,
        )

    halos = [
        halo_copy(0, fbuf, rows, 0, above),
        halo_copy(1, fbuf, HALO, rows + HALO, below),
        halo_copy(2, sbuf, rows, 0, above),
        halo_copy(3, sbuf, HALO, rows + HALO, below),
    ]
    for halo in halos:
        halo.start()

    def patch_copies(source, target, peer):
        return (
            pltpu.make_async_remote_copy(
                src_ref=send_p.at[target, pl.ds(0, 2)],
                dst_ref=recv_p.at[pl.ds(2 * source, 2)],
                send_sem=p_send.at[target],
                recv_sem=p_recv.at[source],
                device_id={"sec": peer},
                device_id_type=pl.DeviceIdType.MESH,
            ),
            pltpu.make_async_remote_copy(
                src_ref=send_p.at[target, 2],
                dst_ref=recv_w.at[source],
                send_sem=w_send.at[target],
                recv_sem=w_recv.at[source],
                device_id={"sec": peer},
                device_id_type=pl.DeviceIdType.MESH,
            ),
        )

    def field_copy(source, target, peer):
        return pltpu.make_async_remote_copy(
            src_ref=send_f.at[target],
            dst_ref=recv_f.at[pl.ds(1 + 2 * source, 2)],
            send_sem=f_send.at[target],
            recv_sem=f_recv.at[source],
            device_id={"sec": peer},
            device_id_type=pl.DeviceIdType.MESH,
        )

    def peer_at(k):
        return lax.rem(me + k, groups)

    @pl.loop(1, groups)
    def _(k):
        peer = peer_at(k)
        for copy in patch_copies(me, peer, peer):
            copy.start()

    def pack(rb, layer, blocks):
        for k in range(4):
            pieces = [
                blocks[c][2 * k : 2 * k + 2, xb * LANES : (xb + 1) * LANES] for c in range(2) for xb in range(2)
            ]
            send_f[4 * rb + k, layer] = jnp.concatenate(pieces, axis=0)

    for layer in range(layers):
        vbuf[:, layer] = plane_steps(
            fbuf[:, layer, pl.ds(HALO, rows), :], sbuf[layer, pl.ds(HALO, rows), :][None]
        )

        @pl.loop(1, rows // 8 - 1)
        def _(rb):
            at = pl.ds(pl.multiple_of(rb * 8, 8), 8)
            pack(rb, layer, [vbuf[c, layer, at, :] for c in range(2)])

    @pl.loop(1, groups)
    def _(k):
        peer = peer_at(k)

        @pl.when((peer >= 4) & (peer < groups - 4))
        def _():
            field_copy(me, peer, peer).start()

    for halo in halos:
        halo.wait_recv()
    for side, base in ((0, 0), (1, rows - HALO)):
        outside = (tile == 0) if side == 0 else (tile == tiles - 1)
        for layer in range(layers):
            force = fbuf[:, layer, pl.ds(base, 3 * HALO), :]
            stiff = sbuf[layer, pl.ds(base, 3 * HALO), :][None]
            row = lax.broadcasted_iota(jnp.int32, force.shape, 1)
            edge = (row < HALO) if side == 0 else (row >= 2 * HALO)
            empty = edge & outside
            force = jnp.where(empty, 0.0, force)
            stiff = jnp.where(empty[:1], 0.0, stiff)
            field = plane_steps(force, stiff)
            pack(0 if side == 0 else rows // 8 - 1, layer, [field[c, HALO : 2 * HALO] for c in range(2)])

    @pl.loop(1, groups)
    def _(k):
        peer = peer_at(k)

        @pl.when((peer < 4) | (peer >= groups - 4))
        def _():
            field_copy(me, peer, peer).start()

    recv_f[pl.ds(1 + 2 * me, 2)] = send_f[me]
    recv_p[pl.ds(2 * me, 2)] = send_p[me, pl.ds(0, 2)]
    recv_w[me] = send_p[me, 2]
    loads[6].wait()

    def both(halves):
        lower = lax.broadcasted_iota(jnp.int32, halves.shape, 1) < 4
        turned = pltpu.roll(halves, 4, 1)
        return jnp.where(lower, halves, turned), jnp.where(lower, turned, halves)

    @pl.loop(0, groups)
    def _(s):
        even, odd = both(zbuf[pl.ds(s, 1)])
        wide_k[pl.ds(2 * s, 1)] = even
        wide_k[pl.ds(2 * s + 1, 1)] = odd

    @pl.loop(1, groups)
    def _(k):
        peer = peer_at(k)
        for copy in patch_copies(peer, peer, me):
            copy.wait_recv()

    @pl.loop(0, groups)
    def _(s):
        even, odd = both(recv_w[pl.ds(s, 1)])
        wide_w[pl.ds(2 * s, 1)] = even
        wide_w[pl.ds(2 * s + 1, 1)] = odd

    @pl.loop(1, groups)
    def _(k):
        peer = peer_at(k)
        field_copy(peer, peer, me).wait_recv()

    chunk = 8
    for step in range(ZSTEPS):
        source, target = (recv_f, other) if step % 2 == 0 else (other, recv_f)

        @pl.loop(0, depth // chunk)
        def _(i):
            z = pl.multiple_of(i * chunk, chunk)
            d = source[pl.ds(z, chunk + 2)]
            slope = d[1:] - d[:-1]
            stretch = recv_p[pl.ds(z, chunk + 1)] - wide_w[pl.ds(z, chunk + 1)] * slope
            bend = wide_k[pl.ds(z, chunk)] * (slope[1:] - slope[:-1])
            target[pl.ds(z + 1, chunk)] = d[1:-1] + STEP_CROSS * (bend + (stretch[:-1] - stretch[1:]))

    final = recv_f if ZSTEPS % 2 == 0 else other

    @pl.loop(0, groups)
    def _(s):
        even, odd = pair_halves(final[pl.ds(1 + 2 * s, 1)], final[pl.ds(2 + 2 * s, 1)])
        out_ref[0, pl.ds(s, 1)] = even
        out_ref[1, pl.ds(s, 1)] = odd

    for halo in halos:
        halo.wait_send()

    @pl.loop(1, groups)
    def _(k):
        peer = peer_at(k)
        for copy in patch_copies(me, peer, peer) + (field_copy(me, peer, peer),):
            copy.wait_send()


def per_device(
    in_plane_force, stiffness, stiffness_z, patch_dest, patch_pos, patch_flow, patch_conf
):
    groups = lax.axis_size("sec")
    _, layers, rows, columns = in_plane_force.shape
    inner_rows = rows // groups
    width = patch_flow.shape[-1]
    blocks = columns // width
    count = patch_pos.shape[2]
    depth = layers * groups
    cross = (
        stiffness_z.reshape(depth, inner_rows, blocks, width)
        .transpose(0, 2, 1, 3)
        .reshape(groups, layers * blocks * inner_rows, width)
    )
    f32, dma = jnp.float32, pltpu.SemaphoreType.DMA
    vmem = pltpu.VMEM
    out = pl.pallas_call(
        body,
        out_shape=jax.ShapeDtypeStruct((2, groups, 8, width), f32),
        in_specs=[pl.BlockSpec(memory_space=pl.ANY)] * 7,
        out_specs=pl.BlockSpec(memory_space=pltpu.VMEM),
        scratch_shapes=[
            vmem((2, layers, rows + 2 * HALO, columns), f32),
            vmem((layers, rows + 2 * HALO, columns), f32),
            vmem((groups, 8, width), f32),
            vmem((1, count), jnp.int32),
            vmem((1, count), jnp.int32),
            vmem((2 * count, width), f32),
            vmem((count, width), f32),
            vmem((2, layers, rows, columns), f32),
            vmem((groups, 3, 8, width), f32),
            vmem((groups, 2, 8, width), f32),
            vmem((depth + 2, 8, width), f32),
            vmem((depth + 1, 8, width), f32),
            vmem((groups, 8, width), f32),
            vmem((depth + 2, 8, width), f32),
            vmem((depth + 1, 8, width), f32),
            vmem((depth, 8, width), f32),
            dma((7,)),
            dma((4,)),
            dma((4,)),
            dma((groups,)),
            dma((groups,)),
            dma((groups,)),
            dma((groups,)),
            dma((groups,)),
            dma((groups,)),
        ],
        compiler_params=pltpu.CompilerParams(collective_id=0, has_side_effects=True),
        name="relax",
    )(
        in_plane_force,
        stiffness,
        cross,
        patch_dest.reshape(1, count),
        patch_pos.reshape(1, count),
        patch_flow.reshape(2 * count, width),
        patch_conf.reshape(count, width),
    )
    return (
        out.reshape(2, depth, blocks, inner_rows, width)
        .transpose(0, 1, 3, 2, 4)
        .reshape(2, depth, inner_rows, columns)
    )


def solution(mesh):
    placed = (
        P(None, "sec", "tile", None),
        P("sec", "tile", None),
        P(None, ("tile", "sec"), None),
        P("sec", "tile", None, None),
        P("sec", "tile", None),
        P("sec", "tile", None, None, None),
        P("sec", "tile", None, None),
    )
    return jax.shard_map(
        per_device,
        mesh=mesh,
        in_specs=placed,
        out_specs=P(None, None, ("tile", "sec"), None),
        check_vma=False,
    )
```

```python
import functools

import jax
import jax.numpy as jnp
from jax import lax
from jax.experimental import pallas as pl
from jax.experimental.pallas import tpu as pltpu
from jax.sharding import PartitionSpec as P

ISTEPS = 8
ZSTEPS = 8
STEP_PLANE = 0.12
STEP_CROSS = 0.15
LANES = 128
HALO = 8
RUN = 4
CHUNK = 16


def plane_steps(force, stiff):
    column = lax.broadcasted_iota(jnp.int32, force.shape, 2)
    first, last = column == 0, column == force.shape[2] - 1
    field = STEP_PLANE * force
    for _ in range(1, ISTEPS):
        up = pltpu.roll(field, 1, 1)
        down = pltpu.roll(field, field.shape[1] - 1, 1)
        left = jnp.where(first, 0.0, pltpu.roll(field, 1, 2))
        right = jnp.where(last, 0.0, pltpu.roll(field, field.shape[2] - 1, 2))
        laplace = (up + down) + (left + right) - 4.0 * field
        field = field + STEP_PLANE * (stiff * laplace + force)
    return field


def split3(value):
    high = value.astype(jnp.bfloat16)
    rest = value - high.astype(jnp.float32)
    middle = rest.astype(jnp.bfloat16)
    low = (rest - middle.astype(jnp.float32)).astype(jnp.bfloat16)
    return high, middle, low


def pair_halves(a, b):
    lower = lax.broadcasted_iota(jnp.int32, a.shape, 1) < 4
    return jnp.where(lower, a, pltpu.roll(b, 4, 1)), jnp.where(lower, pltpu.roll(a, 4, 1), b)


def body(
    force_hbm, stiff_hbm, cross_hbm, dest_hbm, pos_hbm, flow_hbm, conf_hbm, out_ref,
    fbuf, sbuf, zbuf, dest, pos, flow, conf, vbuf,
    send_p, send_f, recv_f, recv_p, other, near, far, bend,
    local_sem, halo_send, halo_recv, p_send, p_recv, f_send, f_recv, ready,
):
    groups = lax.axis_size("sec")
    tiles = lax.axis_size("tile")
    me = lax.axis_index("sec")
    tile = lax.axis_index("tile")
    rows = force_hbm.shape[2]
    layers = force_hbm.shape[1]
    depth = groups * layers
    mesh = pl.DeviceIdType.MESH

    has_side = (tile > 0, tile < tiles - 1)
    neighbour = (lax.rem(tile + tiles - 1, tiles), lax.rem(tile + 1, tiles))
    greets = (lax.rem(tile, RUN) == 0, lax.rem(tile, RUN) != RUN - 1)

    barrier = pltpu.get_barrier_semaphore()

    def peer_at(k):
        return lax.rem(me + k, groups)

    @pl.loop(1, groups)
    def _(k):
        pl.semaphore_signal(barrier, inc=1, device_id={"sec": peer_at(k)}, device_id_type=mesh)

    for side in range(2):

        @pl.when(has_side[side] & greets[side])
        def _():
            pl.semaphore_signal(barrier, inc=1, device_id={"tile": neighbour[side]}, device_id_type=mesh)

    loads = [
        pltpu.make_async_copy(source, target, local_sem.at[i])
        for i, (source, target) in enumerate(
            (
                (dest_hbm, dest),
                (pos_hbm, pos),
                (conf_hbm, conf),
                (flow_hbm, flow),
                (stiff_hbm, sbuf.at[:, pl.ds(HALO, rows), :]),
                (force_hbm, fbuf.at[:, :, pl.ds(HALO, rows), :]),
                (cross_hbm, zbuf),
            )
        )
    ]
    for load in loads:
        load.start()
    for load in loads[:4]:
        load.wait()

    count = conf.shape[0]
    place = pos[...]
    slot = dest[...] * 8 + (place // 4) * 4 + (place % 2) * 2 + (place // 2) % 2
    hot = (lax.broadcasted_iota(jnp.int32, (count, count), 0) == slot).astype(jnp.float32).astype(jnp.bfloat16)
    confidence = conf[...]
    payload = jnp.concatenate(
        [confidence * flow[pl.ds(0, count, stride=2), :], confidence * flow[pl.ds(1, count, stride=2), :], confidence],
        axis=1,
    )
    high, middle, low = [jnp.dot(hot, part, preferred_element_type=jnp.float32) for part in split3(payload)]
    grid = high + middle + low
    pull = [grid[:, c * LANES : (c + 1) * LANES].reshape(groups, 8, LANES) for c in range(2)]
    front, back = pair_halves(*pull)
    send_p[:, 0] = front
    send_p[:, 1] = back
    send_p[:, 2] = grid[:, 2 * LANES :].reshape(groups, 8, LANES)

    blank = jnp.zeros((8, LANES), jnp.float32)
    for buffer in (recv_f, other):
        buffer[0] = blank
        buffer[depth + 1] = blank

    loads[4].wait()
    loads[5].wait()
    waits = groups - 1
    for side in range(2):
        waits = waits + (has_side[side] & jnp.logical_not(greets[side])).astype(jnp.int32)
    pl.semaphore_wait(barrier, waits)

    def halo_copy(index, buffer, side):
        lead = (slice(None),) * (len(buffer.shape) - 2)
        source, target = ((HALO, rows + HALO), (rows, 0))[side]
        return pltpu.make_async_remote_copy(
            src_ref=buffer.at[lead + (pl.ds(source, HALO), slice(None))],
            dst_ref=buffer.at[lead + (pl.ds(target, HALO), slice(None))],
            send_sem=halo_send.at[index, side],
            recv_sem=halo_recv.at[index, 1 - side],
            device_id={"tile": neighbour[side]},
            device_id_type=mesh,
        )

    def halo_copies(side):
        return halo_copy(0, fbuf, side), halo_copy(1, sbuf, side)

    def halo_arrivals(side):
        return halo_copies(1 - side)

    for side in range(2):

        @pl.when(has_side[side] & jnp.logical_not(greets[side]))
        def _():
            pl.semaphore_signal(ready.at[1 - side], inc=1, device_id={"tile": neighbour[side]}, device_id_type=mesh)
            for copy in halo_copies(side):
                copy.start()

    def patch_copy(peer):
        return pltpu.make_async_remote_copy(
            src_ref=send_p.at[peer],
            dst_ref=recv_p.at[me],
            send_sem=p_send,
            recv_sem=p_recv,
            device_id={"sec": peer},
            device_id_type=mesh,
        )

    def field_copy(peer):
        return pltpu.make_async_remote_copy(
            src_ref=send_f.at[peer],
            dst_ref=recv_f.at[pl.ds(1 + 2 * me, 2)],
            send_sem=f_send,
            recv_sem=f_recv,
            device_id={"sec": peer},
            device_id_type=mesh,
        )

    @pl.loop(1, groups)
    def _(k):
        patch_copy(peer_at(k)).start()

    def pack(rb, layer, blocks):
        for k in range(4):
            pieces = [
                blocks[c][2 * k : 2 * k + 2, xb * LANES : (xb + 1) * LANES] for c in range(2) for xb in range(2)
            ]
            send_f[4 * rb + k, layer] = jnp.concatenate(pieces, axis=0)

    for layer in range(layers):
        vbuf[:, layer] = plane_steps(
            fbuf[:, layer, pl.ds(HALO, rows), :], sbuf[layer, pl.ds(HALO, rows), :][None]
        )

        @pl.loop(1, rows // 8 - 1)
        def _(rb):
            at = pl.ds(pl.multiple_of(rb * 8, 8), 8)
            pack(rb, layer, [vbuf[c, layer, at, :] for c in range(2)])

    @pl.loop(1, groups)
    def _(k):
        peer = peer_at(k)

        @pl.when((peer >= 4) & (peer < groups - 4))
        def _():
            field_copy(peer).start()

    for side in (1, 0):

        @pl.when(has_side[side] & greets[side])
        def _():
            pl.semaphore_wait(ready.at[side], 1)
            for copy in halo_copies(side):
                copy.start()

    def both(halves):
        lower = lax.broadcasted_iota(jnp.int32, halves.shape, 1) < 4
        turned = pltpu.roll(halves, 4, 1)
        return jnp.where(lower, halves, turned), jnp.where(lower, turned, halves)

    loads[6].wait()
    recv_p[me] = send_p[me]

    for side, base in ((1, rows - HALO), (0, 0)):

        @pl.when(has_side[side])
        def _():
            for copy in halo_arrivals(side):
                copy.wait_recv()

        for layer in range(layers):
            force = fbuf[:, layer, pl.ds(base, 3 * HALO), :]
            stiff = sbuf[layer, pl.ds(base, 3 * HALO), :][None]
            row = lax.broadcasted_iota(jnp.int32, force.shape, 1)
            edge = (row < HALO) if side == 0 else (row >= 2 * HALO)
            empty = edge & jnp.logical_not(has_side[side])
            force = jnp.where(empty, 0.0, force)
            stiff = jnp.where(empty[:1], 0.0, stiff)
            field = plane_steps(force, stiff)
            pack(0 if side == 0 else rows // 8 - 1, layer, [field[c, HALO : 2 * HALO] for c in range(2)])

        @pl.loop(0, 4)
        def _(k):
            peer = k if side == 0 else groups - 4 + k

            @pl.when(peer != me)
            def _():
                field_copy(peer).start()

    recv_f[pl.ds(1 + 2 * me, 2)] = send_f[me]

    pltpu.make_async_copy(recv_p.at[pl.ds(1, groups - 1)], recv_p.at[pl.ds(1, groups - 1)], p_recv).wait()

    @pl.loop(0, groups - 1)
    def _(s):
        one, two = pl.ds(2 * s, 1), pl.ds(2 * s + 1, 1)
        k_even, k_odd = both(zbuf[pl.ds(s, 1)])
        w_even, w_odd = both(recv_p[pl.ds(s, 1), 2])
        w_next, _ = both(recv_p[pl.ds(s + 1, 1), 2])
        p_even, p_odd, p_next = recv_p[pl.ds(s, 1), 0], recv_p[pl.ds(s, 1), 1], recv_p[pl.ds(s + 1, 1), 0]
        near[one] = STEP_CROSS * (k_even + w_even)
        near[two] = STEP_CROSS * (k_odd + w_odd)
        far[one] = STEP_CROSS * (k_even + w_odd)
        far[two] = STEP_CROSS * (k_odd + w_next)
        bend[one] = STEP_CROSS * (p_even - p_odd)
        bend[two] = STEP_CROSS * (p_odd - p_next)

    k_even, k_odd = both(zbuf[pl.ds(groups - 1, 1)])
    w_even, w_odd = both(recv_p[pl.ds(groups - 1, 1), 2])
    p_even, p_odd = recv_p[pl.ds(groups - 1, 1), 0], recv_p[pl.ds(groups - 1, 1), 1]
    near[pl.ds(depth - 2, 1)] = STEP_CROSS * (k_even + w_even)
    near[pl.ds(depth - 1, 1)] = STEP_CROSS * (k_odd + w_odd)
    far[pl.ds(depth - 2, 1)] = STEP_CROSS * (k_even + w_odd)
    far[pl.ds(depth - 1, 1)] = STEP_CROSS * k_odd
    bend[pl.ds(depth - 2, 1)] = STEP_CROSS * (p_even - p_odd)
    bend[pl.ds(depth - 1, 1)] = STEP_CROSS * p_odd

    pltpu.make_async_copy(recv_f.at[pl.ds(1, depth - 2)], recv_f.at[pl.ds(1, depth - 2)], f_recv).wait()

    for step in range(ZSTEPS):
        source, target = (recv_f, other) if step % 2 == 0 else (other, recv_f)

        @pl.loop(0, depth // CHUNK)
        def _(i):
            z = pl.multiple_of(i * CHUNK, CHUNK)
            d = source[pl.ds(z, CHUNK + 2)]
            slope = d[1:] - d[:-1]
            at = pl.ds(z, CHUNK)
            d = d[1:-1] + ((far[at] * slope[1:] - near[at] * slope[:-1]) + bend[at])
            if step < ZSTEPS - 1:
                target[pl.ds(z + 1, CHUNK)] = d
            else:
                d = d.reshape(CHUNK // 2, 2, 8, LANES)
                even, odd = pair_halves(d[:, 0], d[:, 1])
                half = pl.ds(pl.multiple_of(i * (CHUNK // 2), CHUNK // 2), CHUNK // 2)
                out_ref[0, half] = even
                out_ref[1, half] = odd

    for side in range(2):

        @pl.when(has_side[side])
        def _():
            for copy in halo_copies(side):
                copy.wait_send()

    pltpu.make_async_copy(send_p.at[pl.ds(1, groups - 1)], send_p.at[pl.ds(1, groups - 1)], p_send).wait()
    pltpu.make_async_copy(send_f.at[pl.ds(1, groups - 1)], send_f.at[pl.ds(1, groups - 1)], f_send).wait()


def per_device(
    in_plane_force, stiffness, stiffness_z, patch_dest, patch_pos, patch_flow, patch_conf
):
    groups = lax.axis_size("sec")
    _, layers, rows, columns = in_plane_force.shape
    inner_rows = rows // groups
    width = patch_flow.shape[-1]
    blocks = columns // width
    count = patch_pos.shape[2]
    depth = layers * groups
    cross = (
        stiffness_z.reshape(depth, inner_rows, blocks, width)
        .transpose(0, 2, 1, 3)
        .reshape(groups, layers * blocks * inner_rows, width)
    )
    f32, dma = jnp.float32, pltpu.SemaphoreType.DMA
    vmem = pltpu.VMEM
    out = pl.pallas_call(
        body,
        out_shape=pltpu.VMEM((2, groups, 8, width), f32),
        in_specs=[pl.BlockSpec(memory_space=pl.ANY)] * 7,
        out_specs=pl.BlockSpec(memory_space=pltpu.VMEM),
        scratch_shapes=[
            vmem((2, layers, rows + 2 * HALO, columns), f32),
            vmem((layers, rows + 2 * HALO, columns), f32),
            vmem((groups, 8, width), f32),
            vmem((1, count), jnp.int32),
            vmem((1, count), jnp.int32),
            vmem((2 * count, width), f32),
            vmem((count, width), f32),
            vmem((2, layers, rows, columns), f32),
            vmem((groups, 3, 8, width), f32),
            vmem((groups, 2, 8, width), f32),
            vmem((depth + 2, 8, width), f32),
            vmem((groups, 3, 8, width), f32),
            vmem((depth + 2, 8, width), f32),
            vmem((depth, 8, width), f32),
            vmem((depth, 8, width), f32),
            vmem((depth, 8, width), f32),
            dma((7,)),
            dma((2, 2)),
            dma((2, 2)),
            dma(()),
            dma(()),
            dma(()),
            dma(()),
            pltpu.SemaphoreType.REGULAR((2,)),
        ],
        compiler_params=pltpu.CompilerParams(collective_id=0, has_side_effects=True),
        name="relax",
    )(
        in_plane_force,
        stiffness,
        cross,
        patch_dest.reshape(1, count),
        patch_pos.reshape(1, count),
        patch_flow.reshape(2 * count, width),
        patch_conf.reshape(count, width),
    )
    return (
        out.reshape(2, depth, blocks, inner_rows, width)
        .transpose(0, 1, 3, 2, 4)
        .reshape(2, depth, inner_rows, columns)
    )


def solution(mesh):
    placed = (
        P(None, "sec", "tile", None),
        P("sec", "tile", None),
        P(None, ("tile", "sec"), None),
        P("sec", "tile", None, None),
        P("sec", "tile", None),
        P("sec", "tile", None, None, None),
        P("sec", "tile", None, None),
    )
    return jax.shard_map(
        per_device,
        mesh=mesh,
        in_specs=placed,
        out_specs=P(None, None, ("tile", "sec"), None),
        check_vma=False,
    )
```

```python
import functools

import jax
import jax.numpy as jnp
from jax import lax
from jax.experimental import pallas as pl
from jax.experimental.pallas import tpu as pltpu
from jax.sharding import PartitionSpec as P

ISTEPS = 8
ZSTEPS = 8
STEP_PLANE = 0.12
STEP_CROSS = 0.15
LANES = 128
HALO = 8
RUN = 4
CHUNK = 32


def plane_steps(force, stiff):
    column = lax.broadcasted_iota(jnp.int32, force.shape, 2)
    first, last = column == 0, column == force.shape[2] - 1
    field = STEP_PLANE * force
    for _ in range(1, ISTEPS):
        up = pltpu.roll(field, 1, 1)
        down = pltpu.roll(field, field.shape[1] - 1, 1)
        left = jnp.where(first, 0.0, pltpu.roll(field, 1, 2))
        right = jnp.where(last, 0.0, pltpu.roll(field, field.shape[2] - 1, 2))
        laplace = (up + down) + (left + right) - 4.0 * field
        field = field + STEP_PLANE * (stiff * laplace + force)
    return field


def split3(value):
    high = value.astype(jnp.bfloat16)
    rest = value - high.astype(jnp.float32)
    middle = rest.astype(jnp.bfloat16)
    low = (rest - middle.astype(jnp.float32)).astype(jnp.bfloat16)
    return high, middle, low


def pair_halves(a, b):
    lower = lax.broadcasted_iota(jnp.int32, a.shape, 1) < 4
    return jnp.where(lower, a, pltpu.roll(b, 4, 1)), jnp.where(lower, pltpu.roll(a, 4, 1), b)


def body(
    force_hbm, stiff_hbm, cross_hbm, dest_hbm, pos_hbm, flow_hbm, conf_hbm, out_ref,
    fbuf, sbuf, zbuf, dest, pos, flow, conf, vbuf,
    send_p, send_f, recv_f, recv_p, other, near, far, bend,
    local_sem, halo_send, halo_recv, p_send, p_recv, f_send, f_recv, ready, met,
):
    groups = lax.axis_size("sec")
    tiles = lax.axis_size("tile")
    me = lax.axis_index("sec")
    tile = lax.axis_index("tile")
    rows = force_hbm.shape[2]
    layers = force_hbm.shape[1]
    depth = groups * layers
    mesh = pl.DeviceIdType.MESH

    has_side = (tile > 0, tile < tiles - 1)
    neighbour = (lax.rem(tile + tiles - 1, tiles), lax.rem(tile + 1, tiles))
    greets = (lax.rem(tile, RUN) == 0, lax.rem(tile, RUN) != RUN - 1)

    barrier = pltpu.get_barrier_semaphore()

    core = lax.rem(me, 2)
    partner = me + 1 - 2 * core

    half = groups // 2
    split = lax.rem(tile, RUN) < RUN // 2

    direct = lax.rem(tile, RUN) == RUN // 2

    def in_first(peer):
        return split & (peer > 0) & (peer < half)

    def peer_at(k):
        away = lax.rem(me + jnp.where(core == 0, k, groups - k), groups)
        level = jnp.where(split, k // 8, groups // 8 - 1 - k // 8)
        return jnp.where(split | direct, level * 8 + lax.rem(me + k, 8), away)

    first = in_first(me)

    @pl.loop(0, half)
    def _(k):
        collector = 2 * lax.rem(me // 2 + k, half) + 1 - first.astype(jnp.int32)

        @pl.when(collector != me)
        def _():
            pl.semaphore_signal(barrier, inc=1, device_id={"sec": collector}, device_id_type=mesh)

    @pl.when((core == 1) & jnp.logical_not(first))
    def _():
        pl.semaphore_signal(barrier, inc=1, device_id={"sec": partner}, device_id_type=mesh)

    for side in range(2):

        @pl.when(has_side[side] & greets[side])
        def _():
            target = {"sec": me - core, "tile": neighbour[side]}
            pl.semaphore_signal(barrier, inc=1, device_id=target, device_id_type=mesh)

    loads = [
        pltpu.make_async_copy(source, target, local_sem.at[i])
        for i, (source, target) in enumerate(
            (
                (dest_hbm, dest),
                (pos_hbm, pos),
                (conf_hbm, conf),
                (flow_hbm, flow),
                (stiff_hbm, sbuf.at[:, pl.ds(HALO, rows), :]),
                (force_hbm, fbuf.at[:, :, pl.ds(HALO, rows), :]),
                (cross_hbm, zbuf),
            )
        )
    ]
    def halo_copy(index, buffer, side):
        lead = (slice(None),) * (len(buffer.shape) - 2)
        reach = ISTEPS - 1 - index
        source, target = ((HALO, rows + HALO), (rows + HALO - reach, HALO - reach))[side]
        return pltpu.make_async_remote_copy(
            src_ref=buffer.at[lead + (pl.ds(source, reach), slice(None))],
            dst_ref=buffer.at[lead + (pl.ds(target, reach), slice(None))],
            send_sem=halo_send.at[index, side],
            recv_sem=halo_recv.at[index, 1 - side],
            device_id={"tile": neighbour[side]},
            device_id_type=mesh,
        )

    def halo_copies(side):
        return halo_copy(0, fbuf, side), halo_copy(1, sbuf, side)

    def meet():
        @pl.when(core == 0)
        def _():
            members = half - 1 - first.astype(jnp.int32)
            waits = jnp.where(split, members, 0) + (partner >= half).astype(jnp.int32)
            waits = jnp.where(split, waits, 1)
            for side in range(2):
                waits = waits + 2 * (has_side[side] & jnp.logical_not(greets[side])).astype(jnp.int32)
            pl.semaphore_wait(barrier, waits)
            pl.semaphore_signal(met, inc=1, device_id={"sec": partner}, device_id_type=mesh)

        @pl.when(core == 1)
        def _():
            pl.semaphore_wait(met, 1)

        for side in range(2):

            @pl.when(has_side[side] & jnp.logical_not(greets[side]))
            def _():
                pl.semaphore_signal(ready.at[1 - side], inc=1, device_id={"tile": neighbour[side]}, device_id_type=mesh)
                for copy in halo_copies(side):
                    copy.start()

    for load in loads[4:6] + loads[:4] + loads[6:]:
        load.start()
    loads[4].wait()
    loads[5].wait()
    pl.when(jnp.logical_not(split))(meet)
    for load in loads[:4]:
        load.wait()

    count = conf.shape[0]
    place = pos[...]
    slot = dest[...] * 8 + (place // 4) * 4 + (place % 2) * 2 + (place // 2) % 2
    hot = (lax.broadcasted_iota(jnp.int32, (count, count), 0) == slot).astype(jnp.float32).astype(jnp.bfloat16)
    confidence = conf[...]
    payload = jnp.concatenate(
        [confidence * flow[pl.ds(0, count, stride=2), :], confidence * flow[pl.ds(1, count, stride=2), :], confidence],
        axis=1,
    )
    high, middle, low = [jnp.dot(hot, part, preferred_element_type=jnp.float32) for part in split3(payload)]
    grid = high + middle + low
    pull = [grid[:, c * LANES : (c + 1) * LANES].reshape(groups, 8, LANES) for c in range(2)]
    front, back = pair_halves(*pull)
    send_p[:, 0] = front
    send_p[:, 1] = back
    send_p[:, 2] = grid[:, 2 * LANES :].reshape(groups, 8, LANES)

    blank = jnp.zeros((8, LANES), jnp.float32)
    for buffer in (recv_f, other):
        buffer[0] = blank
        buffer[depth + 1] = blank

    pl.when(split)(meet)

    def patch_copy(peer):
        return pltpu.make_async_remote_copy(
            src_ref=send_p.at[peer],
            dst_ref=recv_p.at[me],
            send_sem=p_send,
            recv_sem=p_recv,
            device_id={"sec": peer},
            device_id_type=mesh,
        )

    def field_copy(peer):
        return pltpu.make_async_remote_copy(
            src_ref=send_f.at[peer],
            dst_ref=recv_f.at[pl.ds(1 + 2 * me, 2)],
            send_sem=f_send,
            recv_sem=f_recv,
            device_id={"sec": peer},
            device_id_type=mesh,
        )

    def answer(when):
        for side in (1, 0):

            @pl.when(when & has_side[side] & greets[side])
            def _():
                pl.semaphore_wait(ready.at[side], 1)
                for copy in halo_copies(side):
                    copy.start()

    @pl.when(split)
    def _():
        @pl.loop(0, half)
        def _(k):
            peer = peer_at(k)

            @pl.when(in_first(peer) & (peer != me))
            def _():
                patch_copy(peer).start()

    def pack(rb, layer, blocks):
        for k in range(4):
            pieces = [
                blocks[c][2 * k : 2 * k + 2, xb * LANES : (xb + 1) * LANES] for c in range(2) for xb in range(2)
            ]
            send_f[4 * rb + k, layer] = jnp.concatenate(pieces, axis=0)

    for layer in range(layers):
        vbuf[:, layer] = plane_steps(
            fbuf[:, layer, pl.ds(HALO, rows), :], sbuf[layer, pl.ds(HALO, rows), :][None]
        )

        @pl.loop(1, rows // 8 - 1)
        def _(rb):
            at = pl.ds(pl.multiple_of(rb * 8, 8), 8)
            pack(rb, layer, [vbuf[c, layer, at, :] for c in range(2)])

    @pl.when(core == 1)
    def _():
        others = jnp.where(split, half + 1, groups)
        pl.semaphore_wait(barrier, others - (jnp.logical_not(first)).astype(jnp.int32))
        pl.semaphore_signal(met, inc=1, device_id={"sec": partner}, device_id_type=mesh)

    @pl.when(core == 0)
    def _():
        pl.semaphore_wait(met, 1)

    answer(direct)

    def send_patches(low, high):
        @pl.loop(low, high)
        def _(k):
            peer = peer_at(k)

            @pl.when(jnp.logical_not(in_first(peer)) & (peer != me))
            def _():
                patch_copy(peer).start()

    send_patches(0, groups)
    answer(jnp.logical_not(direct))

    def send_inner(low, high, late):
        @pl.loop(low, high)
        def _(k):
            peer = peer_at(k)
            held = split & (lax.rem(peer, 8) < 4)

            @pl.when((peer >= 4) & (peer < groups - 4) & (peer != me) & (held == late))
            def _():
                field_copy(peer).start()

    send_inner(0, half, False)

    def both(halves):
        lower = lax.broadcasted_iota(jnp.int32, halves.shape, 1) < 4
        turned = pltpu.roll(halves, 4, 1)
        return jnp.where(lower, halves, turned), jnp.where(lower, turned, halves)

    loads[6].wait()
    recv_p[me] = send_p[me]

    lead = lax.rem(tile, RUN) == 0

    @pl.loop(0, 2)
    def _(turn):
        side = jnp.where(lead, turn, 1 - turn)
        inside = jnp.where(side == 0, tile > 0, tile < tiles - 1)
        base = pl.multiple_of(side * (rows - HALO), HALO)

        @pl.when(inside)
        def _():
            for index, buffer in enumerate((fbuf, sbuf)):
                reach = ISTEPS - 1 - index
                block = buffer.at[(slice(None),) * (len(buffer.shape) - 2) + (pl.ds(HALO, reach), slice(None))]
                pltpu.make_async_copy(block, block, halo_recv.at[index, side]).wait()

        for layer in range(layers):
            force = fbuf[:, layer, pl.ds(base, 3 * HALO), :]
            stiff = sbuf[layer, pl.ds(base, 3 * HALO), :][None]
            row = lax.broadcasted_iota(jnp.int32, force.shape, 1)
            edge = jnp.where(side == 0, row, 3 * HALO - 1 - row) < HALO
            empty = edge & jnp.logical_not(inside)
            force = jnp.where(empty, 0.0, force)
            stiff = jnp.where(empty[:1], 0.0, stiff)
            field = plane_steps(force, stiff)
            pack(side * (rows // 8 - 1), layer, [field[c, HALO : 2 * HALO] for c in range(2)])

        @pl.loop(0, 4)
        def _(k):
            peer = k + side * (groups - 4)

            @pl.when(peer != me)
            def _():
                field_copy(peer).start()

    send_inner(0, half, True)
    send_inner(half, groups, False)
    send_inner(half, groups, True)

    recv_f[pl.ds(1 + 2 * me, 2)] = send_f[me]

    pltpu.make_async_copy(recv_p.at[pl.ds(1, groups - 1)], recv_p.at[pl.ds(1, groups - 1)], p_recv).wait()

    @pl.loop(0, groups - 1)
    def _(s):
        one, two = pl.ds(2 * s, 1), pl.ds(2 * s + 1, 1)
        k_even, k_odd = both(zbuf[pl.ds(s, 1)])
        w_even, w_odd = both(recv_p[pl.ds(s, 1), 2])
        w_next, _ = both(recv_p[pl.ds(s + 1, 1), 2])
        p_even, p_odd, p_next = recv_p[pl.ds(s, 1), 0], recv_p[pl.ds(s, 1), 1], recv_p[pl.ds(s + 1, 1), 0]
        near[one] = STEP_CROSS * (k_even + w_even)
        near[two] = STEP_CROSS * (k_odd + w_odd)
        far[one] = STEP_CROSS * (k_even + w_odd)
        far[two] = STEP_CROSS * (k_odd + w_next)
        bend[one] = STEP_CROSS * (p_even - p_odd)
        bend[two] = STEP_CROSS * (p_odd - p_next)

    k_even, k_odd = both(zbuf[pl.ds(groups - 1, 1)])
    w_even, w_odd = both(recv_p[pl.ds(groups - 1, 1), 2])
    p_even, p_odd = recv_p[pl.ds(groups - 1, 1), 0], recv_p[pl.ds(groups - 1, 1), 1]
    near[pl.ds(depth - 2, 1)] = STEP_CROSS * (k_even + w_even)
    near[pl.ds(depth - 1, 1)] = STEP_CROSS * (k_odd + w_odd)
    far[pl.ds(depth - 2, 1)] = STEP_CROSS * (k_even + w_odd)
    far[pl.ds(depth - 1, 1)] = STEP_CROSS * k_odd
    bend[pl.ds(depth - 2, 1)] = STEP_CROSS * (p_even - p_odd)
    bend[pl.ds(depth - 1, 1)] = STEP_CROSS * p_odd

    pltpu.make_async_copy(recv_f.at[pl.ds(1, depth - 2)], recv_f.at[pl.ds(1, depth - 2)], f_recv).wait()

    for step in range(ZSTEPS):
        source, target = (recv_f, other) if step % 2 == 0 else (other, recv_f)

        @pl.loop(0, depth // CHUNK)
        def _(i):
            z = pl.multiple_of(i * CHUNK, CHUNK)
            d = source[pl.ds(z, CHUNK + 2)]
            slope = d[1:] - d[:-1]
            at = pl.ds(z, CHUNK)
            d = d[1:-1] + ((far[at] * slope[1:] - near[at] * slope[:-1]) + bend[at])
            if step < ZSTEPS - 1:
                target[pl.ds(z + 1, CHUNK)] = d
            else:
                d = d.reshape(CHUNK // 2, 2, 8, LANES)
                even, odd = pair_halves(d[:, 0], d[:, 1])
                half = pl.ds(pl.multiple_of(i * (CHUNK // 2), CHUNK // 2), CHUNK // 2)
                out_ref[0, half] = even
                out_ref[1, half] = odd

    for side in range(2):

        @pl.when(has_side[side])
        def _():
            for copy in halo_copies(side):
                copy.wait_send()

    pltpu.make_async_copy(send_p.at[pl.ds(1, groups - 1)], send_p.at[pl.ds(1, groups - 1)], p_send).wait()
    pltpu.make_async_copy(send_f.at[pl.ds(1, groups - 1)], send_f.at[pl.ds(1, groups - 1)], f_send).wait()


def per_device(
    in_plane_force, stiffness, stiffness_z, patch_dest, patch_pos, patch_flow, patch_conf
):
    groups = lax.axis_size("sec")
    _, layers, rows, columns = in_plane_force.shape
    inner_rows = rows // groups
    width = patch_flow.shape[-1]
    blocks = columns // width
    count = patch_pos.shape[2]
    depth = layers * groups
    cross = (
        stiffness_z.reshape(depth, inner_rows, blocks, width)
        .transpose(0, 2, 1, 3)
        .reshape(groups, layers * blocks * inner_rows, width)
    )
    f32, dma = jnp.float32, pltpu.SemaphoreType.DMA
    vmem = pltpu.VMEM
    out = pl.pallas_call(
        body,
        out_shape=pltpu.VMEM((2, groups, 8, width), f32),
        in_specs=[pl.BlockSpec(memory_space=pl.ANY)] * 7,
        out_specs=pl.BlockSpec(memory_space=pltpu.VMEM),
        scratch_shapes=[
            vmem((2, layers, rows + 2 * HALO, columns), f32),
            vmem((layers, rows + 2 * HALO, columns), f32),
            vmem((groups, 8, width), f32),
            vmem((1, count), jnp.int32),
            vmem((1, count), jnp.int32),
            vmem((2 * count, width), f32),
            vmem((count, width), f32),
            vmem((2, layers, rows, columns), f32),
            vmem((groups, 3, 8, width), f32),
            vmem((groups, 2, 8, width), f32),
            vmem((depth + 2, 8, width), f32),
            vmem((groups, 3, 8, width), f32),
            vmem((depth + 2, 8, width), f32),
            vmem((depth, 8, width), f32),
            vmem((depth, 8, width), f32),
            vmem((depth, 8, width), f32),
            dma((7,)),
            dma((2, 2)),
            dma((2, 2)),
            dma(()),
            dma(()),
            dma(()),
            dma(()),
            pltpu.SemaphoreType.REGULAR((2,)),
            pltpu.SemaphoreType.REGULAR,
        ],
        compiler_params=pltpu.CompilerParams(collective_id=0, has_side_effects=True),
        name="relax",
    )(
        in_plane_force,
        stiffness,
        cross,
        patch_dest.reshape(1, count),
        patch_pos.reshape(1, count),
        patch_flow.reshape(2 * count, width),
        patch_conf.reshape(count, width),
    )
    return (
        out.reshape(2, depth, blocks, inner_rows, width)
        .transpose(0, 1, 3, 2, 4)
        .reshape(2, depth, inner_rows, columns)
    )


def solution(mesh):
    placed = (
        P(None, "sec", "tile", None),
        P("sec", "tile", None),
        P(None, ("tile", "sec"), None),
        P("sec", "tile", None, None),
        P("sec", "tile", None),
        P("sec", "tile", None, None, None),
        P("sec", "tile", None, None),
    )
    return jax.shard_map(
        per_device,
        mesh=mesh,
        in_specs=placed,
        out_specs=P(None, None, ("tile", "sec"), None),
        check_vma=False,
    )
```

```python
import functools

import jax
import jax.numpy as jnp
from jax import lax
from jax.experimental import pallas as pl
from jax.experimental.pallas import tpu as pltpu
from jax.sharding import PartitionSpec as P

ISTEPS = 8
ZSTEPS = 8
STEP_PLANE = 0.12
STEP_CROSS = 0.15
LANES = 128
HALO = 8
RUN = 4
CHUNK = 32
DEFER = 24


def plane_steps(force, stiff):
    y, x = force.ndim - 2, force.ndim - 1
    rows, columns = force.shape[y:]
    column = lax.broadcasted_iota(jnp.int32, force.shape, x)
    first, last = column == 0, column == columns - 1
    field = STEP_PLANE * force
    for _ in range(1, ISTEPS):
        up = pltpu.roll(field, 1, y)
        down = pltpu.roll(field, rows - 1, y)
        left = jnp.where(first, 0.0, pltpu.roll(field, 1, x))
        right = jnp.where(last, 0.0, pltpu.roll(field, columns - 1, x))
        laplace = (up + down) + (left + right) - 4.0 * field
        field = field + STEP_PLANE * (stiff * laplace + force)
    return field


def split3(value):
    high = value.astype(jnp.bfloat16)
    rest = value - high.astype(jnp.float32)
    middle = rest.astype(jnp.bfloat16)
    low = (rest - middle.astype(jnp.float32)).astype(jnp.bfloat16)
    return high, middle, low


def pair_halves(a, b):
    lower = lax.broadcasted_iota(jnp.int32, a.shape, 1) < 4
    return jnp.where(lower, a, pltpu.roll(b, 4, 1)), jnp.where(lower, pltpu.roll(a, 4, 1), b)


def body(
    force_hbm, stiff_hbm, cross_hbm, dest_hbm, pos_hbm, flow_hbm, conf_hbm, out_ref,
    fbuf, sbuf, zbuf, dest, pos, flow, conf, vbuf,
    send_p, send_f, recv_f, recv_p, other, near, far, bend,
    local_sem, halo_send, halo_recv, p_send, p_recv, f_send, f_recv, ready, met,
):
    groups = lax.axis_size("sec")
    tiles = lax.axis_size("tile")
    me = lax.axis_index("sec")
    tile = lax.axis_index("tile")
    rows = force_hbm.shape[2]
    layers = force_hbm.shape[1]
    depth = groups * layers
    mesh = pl.DeviceIdType.MESH

    has_side = (tile > 0, tile < tiles - 1)
    neighbour = (lax.rem(tile + tiles - 1, tiles), lax.rem(tile + 1, tiles))
    greets = (lax.rem(tile, RUN) == 0, lax.rem(tile, RUN) != RUN - 1)

    barrier = pltpu.get_barrier_semaphore()

    core = lax.rem(me, 2)
    partner = me + 1 - 2 * core

    half = groups // 2
    split = lax.rem(tile, RUN) < RUN // 2

    direct = lax.rem(tile, RUN) == RUN // 2

    def in_first(peer):
        return split & (peer > 0) & (peer < half)

    def peer_at(k):
        away = lax.rem(me + jnp.where(core == 0, k, groups - k), groups)
        level = jnp.where(split, k // 8, groups // 8 - 1 - k // 8)
        return jnp.where(split | direct, level * 8 + lax.rem(me + k, 8), away)

    first = in_first(me)

    @pl.when((core == 1) & jnp.logical_not(first))
    def _():
        pl.semaphore_signal(barrier, inc=1, device_id={"sec": partner}, device_id_type=mesh)

    for side in range(2):

        @pl.when(has_side[side] & greets[side])
        def _():
            target = {"sec": me - core, "tile": neighbour[side]}
            pl.semaphore_signal(barrier, inc=1, device_id=target, device_id_type=mesh)

    @pl.loop(0, half)
    def _(k):
        collector = 2 * lax.rem(me // 2 + k, half) + 1 - first.astype(jnp.int32)

        @pl.when(collector != me)
        def _():
            pl.semaphore_signal(barrier, inc=1, device_id={"sec": collector}, device_id_type=mesh)

    loads = [
        pltpu.make_async_copy(source, target, local_sem.at[i])
        for i, (source, target) in enumerate(
            (
                (dest_hbm, dest),
                (pos_hbm, pos),
                (conf_hbm, conf),
                (flow_hbm, flow),
                (stiff_hbm, sbuf.at[:, pl.ds(HALO, rows), :]),
                (force_hbm, fbuf.at[:, :, pl.ds(HALO, rows), :]),
                (cross_hbm, zbuf),
            )
        )
    ]
    def halo_copy(index, values, buffer, side):
        lead = (slice(None),) * (len(buffer.shape) - 2)
        reach = ISTEPS - 1 - index
        source, target = ((0, rows + HALO), (rows - reach, HALO - reach))[side]
        return pltpu.make_async_remote_copy(
            src_ref=values.at[lead + (pl.ds(source, reach), slice(None))],
            dst_ref=buffer.at[lead + (pl.ds(target, reach), slice(None))],
            send_sem=halo_send.at[index, side],
            recv_sem=halo_recv.at[index, 1 - side],
            device_id={"tile": neighbour[side]},
            device_id_type=mesh,
        )

    def halo_copies(side):
        return halo_copy(0, force_hbm, fbuf, side), halo_copy(1, stiff_hbm, sbuf, side)

    def meet():
        @pl.when(core == 0)
        def _():
            members = half - 1 - first.astype(jnp.int32)
            waits = jnp.where(split, members, 0) + (partner >= half).astype(jnp.int32)
            waits = jnp.where(split, waits, 1)
            for side in range(2):
                waits = waits + 2 * (has_side[side] & jnp.logical_not(greets[side])).astype(jnp.int32)
            pl.semaphore_wait(barrier, waits)
            pl.semaphore_signal(met, inc=1, device_id={"sec": partner}, device_id_type=mesh)

        @pl.when(core == 1)
        def _():
            pl.semaphore_wait(met, 1)

        for side in range(2):

            @pl.when(has_side[side] & jnp.logical_not(greets[side]))
            def _():
                pl.semaphore_signal(ready.at[1 - side], inc=1, device_id={"tile": neighbour[side]}, device_id_type=mesh)
                for copy in halo_copies(side):
                    copy.start()

    for load in loads:
        load.start()
    pl.when(jnp.logical_not(split))(meet)
    for load in loads[:6]:
        load.wait()

    count = conf.shape[0]
    place = pos[...]
    slot = dest[...] * 8 + (place // 4) * 4 + (place % 2) * 2 + (place // 2) % 2
    hot = (lax.broadcasted_iota(jnp.int32, (count, count), 0) == slot).astype(jnp.float32).astype(jnp.bfloat16)
    confidence = conf[...]
    payload = jnp.concatenate(
        [confidence * flow[pl.ds(0, count, stride=2), :], confidence * flow[pl.ds(1, count, stride=2), :], confidence],
        axis=1,
    )
    high, middle, low = [jnp.dot(hot, part, preferred_element_type=jnp.float32) for part in split3(payload)]
    grid = high + middle + low
    pull = [grid[:, c * LANES : (c + 1) * LANES].reshape(groups, 8, LANES) for c in range(2)]
    front, back = pair_halves(*pull)
    send_p[:, 0] = front
    send_p[:, 1] = back
    send_p[:, 2] = grid[:, 2 * LANES :].reshape(groups, 8, LANES)

    blank = jnp.zeros((8, LANES), jnp.float32)
    for buffer in (recv_f, other):
        buffer[0] = blank
        buffer[depth + 1] = blank

    pl.when(split)(meet)

    def patch_copy(peer):
        return pltpu.make_async_remote_copy(
            src_ref=send_p.at[peer],
            dst_ref=recv_p.at[me],
            send_sem=p_send,
            recv_sem=p_recv,
            device_id={"sec": peer},
            device_id_type=mesh,
        )

    def field_copy(peer):
        return pltpu.make_async_remote_copy(
            src_ref=send_f.at[peer],
            dst_ref=recv_f.at[pl.ds(1 + 2 * me, 2)],
            send_sem=f_send,
            recv_sem=f_recv,
            device_id={"sec": peer},
            device_id_type=mesh,
        )

    def answer(when):
        for side in (1, 0):

            @pl.when(when & has_side[side] & greets[side])
            def _():
                pl.semaphore_wait(ready.at[side], 1)
                for copy in halo_copies(side):
                    copy.start()

    @pl.when(split)
    def _():
        @pl.loop(0, half)
        def _(k):
            peer = peer_at(k)

            @pl.when(in_first(peer) & (peer != me))
            def _():
                patch_copy(peer).start()

    def pack(rb, layer, blocks):
        for k in range(4):
            pieces = [
                blocks[c][2 * k : 2 * k + 2, xb * LANES : (xb + 1) * LANES] for c in range(2) for xb in range(2)
            ]
            send_f[4 * rb + k, layer] = jnp.concatenate(pieces, axis=0)

    for layer in range(layers):
        vbuf[:, layer] = plane_steps(
            fbuf[:, layer, pl.ds(HALO, rows), :], sbuf[layer, pl.ds(HALO, rows), :][None]
        )

        @pl.loop(1, rows // 8 - 1)
        def _(rb):
            at = pl.ds(pl.multiple_of(rb * 8, 8), 8)
            pack(rb, layer, [vbuf[c, layer, at, :] for c in range(2)])

    @pl.when(core == 1)
    def _():
        others = jnp.where(split, half + 1, groups)
        pl.semaphore_wait(barrier, others - (jnp.logical_not(first)).astype(jnp.int32))
        pl.semaphore_signal(met, inc=1, device_id={"sec": partner}, device_id_type=mesh)

    @pl.when(core == 0)
    def _():
        pl.semaphore_wait(met, 1)

    answer(direct)

    def send_patches(low, high):
        @pl.loop(low, high)
        def _(k):
            peer = peer_at(k)

            @pl.when(jnp.logical_not(in_first(peer)) & (peer != me))
            def _():
                patch_copy(peer).start()

    send_patches(0, DEFER)
    answer(jnp.logical_not(direct))
    send_patches(DEFER, groups)

    def send_inner(late):
        @pl.loop(0, groups)
        def _(k):
            peer = peer_at(k)
            held = (lax.rem(peer, 8) < 4) == (peer < half)

            @pl.when((peer >= 4) & (peer < groups - 4) & (peer != me) & (held == late))
            def _():
                field_copy(peer).start()

    send_inner(False)

    def both(halves):
        lower = lax.broadcasted_iota(jnp.int32, halves.shape, 1) < 4
        turned = pltpu.roll(halves, 4, 1)
        return jnp.where(lower, halves, turned), jnp.where(lower, turned, halves)

    loads[6].wait()
    recv_p[me] = send_p[me]

    lead = (lax.rem(tile, RUN) == 0) | (lax.rem(tile, RUN) == RUN - 1)

    @pl.loop(0, 2)
    def _(turn):
        side = jnp.where(lead, turn, 1 - turn)
        inside = jnp.where(side == 0, tile > 0, tile < tiles - 1)
        base = pl.multiple_of(side * (rows - HALO), HALO)

        @pl.when(inside)
        def _():
            for index, buffer in enumerate((fbuf, sbuf)):
                reach = ISTEPS - 1 - index
                block = buffer.at[(slice(None),) * (len(buffer.shape) - 2) + (pl.ds(HALO, reach), slice(None))]
                pltpu.make_async_copy(block, block, halo_recv.at[index, side]).wait()

        force = fbuf[:, :, pl.ds(base, 3 * HALO), :]
        stiff = sbuf[:, pl.ds(base, 3 * HALO), :][None]
        row = lax.broadcasted_iota(jnp.int32, force.shape, 2)
        edge = jnp.where(side == 0, row, 3 * HALO - 1 - row) < HALO
        empty = edge & jnp.logical_not(inside)
        force = jnp.where(empty, 0.0, force)
        stiff = jnp.where(empty[:1], 0.0, stiff)
        field = plane_steps(force, stiff)
        for layer in range(layers):
            pack(side * (rows // 8 - 1), layer, [field[c, layer, HALO : 2 * HALO] for c in range(2)])

        @pl.loop(0, 4)
        def _(k):
            peer = k + side * (groups - 4)

            @pl.when(peer != me)
            def _():
                field_copy(peer).start()

    send_inner(True)

    recv_f[pl.ds(1 + 2 * me, 2)] = send_f[me]

    pltpu.make_async_copy(recv_p.at[pl.ds(1, groups - 1)], recv_p.at[pl.ds(1, groups - 1)], p_recv).wait()

    @pl.loop(0, groups - 1)
    def _(s):
        one, two = pl.ds(2 * s, 1), pl.ds(2 * s + 1, 1)
        k_even, k_odd = both(zbuf[pl.ds(s, 1)])
        w_even, w_odd = both(recv_p[pl.ds(s, 1), 2])
        w_next, _ = both(recv_p[pl.ds(s + 1, 1), 2])
        p_even, p_odd, p_next = recv_p[pl.ds(s, 1), 0], recv_p[pl.ds(s, 1), 1], recv_p[pl.ds(s + 1, 1), 0]
        near[one] = STEP_CROSS * (k_even + w_even)
        near[two] = STEP_CROSS * (k_odd + w_odd)
        far[one] = STEP_CROSS * (k_even + w_odd)
        far[two] = STEP_CROSS * (k_odd + w_next)
        bend[one] = STEP_CROSS * (p_even - p_odd)
        bend[two] = STEP_CROSS * (p_odd - p_next)

    k_even, k_odd = both(zbuf[pl.ds(groups - 1, 1)])
    w_even, w_odd = both(recv_p[pl.ds(groups - 1, 1), 2])
    p_even, p_odd = recv_p[pl.ds(groups - 1, 1), 0], recv_p[pl.ds(groups - 1, 1), 1]
    near[pl.ds(depth - 2, 1)] = STEP_CROSS * (k_even + w_even)
    near[pl.ds(depth - 1, 1)] = STEP_CROSS * (k_odd + w_odd)
    far[pl.ds(depth - 2, 1)] = STEP_CROSS * (k_even + w_odd)
    far[pl.ds(depth - 1, 1)] = STEP_CROSS * k_odd
    bend[pl.ds(depth - 2, 1)] = STEP_CROSS * (p_even - p_odd)
    bend[pl.ds(depth - 1, 1)] = STEP_CROSS * p_odd

    pltpu.make_async_copy(recv_f.at[pl.ds(1, depth - 2)], recv_f.at[pl.ds(1, depth - 2)], f_recv).wait()

    for step in range(ZSTEPS):
        source, target = (recv_f, other) if step % 2 == 0 else (other, recv_f)

        @pl.loop(0, depth // CHUNK)
        def _(i):
            z = pl.multiple_of(i * CHUNK, CHUNK)
            d = source[pl.ds(z, CHUNK + 2)]
            slope = d[1:] - d[:-1]
            at = pl.ds(z, CHUNK)
            d = d[1:-1] + ((far[at] * slope[1:] - near[at] * slope[:-1]) + bend[at])
            if step < ZSTEPS - 1:
                target[pl.ds(z + 1, CHUNK)] = d
            else:
                d = d.reshape(CHUNK // 2, 2, 8, LANES)
                even, odd = pair_halves(d[:, 0], d[:, 1])
                half = pl.ds(pl.multiple_of(i * (CHUNK // 2), CHUNK // 2), CHUNK // 2)
                out_ref[0, half] = even
                out_ref[1, half] = odd

    for side in range(2):

        @pl.when(has_side[side])
        def _():
            for copy in halo_copies(side):
                copy.wait_send()

    pltpu.make_async_copy(send_p.at[pl.ds(1, groups - 1)], send_p.at[pl.ds(1, groups - 1)], p_send).wait()
    pltpu.make_async_copy(send_f.at[pl.ds(1, groups - 1)], send_f.at[pl.ds(1, groups - 1)], f_send).wait()


def per_device(
    in_plane_force, stiffness, stiffness_z, patch_dest, patch_pos, patch_flow, patch_conf
):
    groups = lax.axis_size("sec")
    _, layers, rows, columns = in_plane_force.shape
    inner_rows = rows // groups
    width = patch_flow.shape[-1]
    blocks = columns // width
    count = patch_pos.shape[2]
    depth = layers * groups
    cross = (
        stiffness_z.reshape(depth, inner_rows, blocks, width)
        .transpose(0, 2, 1, 3)
        .reshape(groups, layers * blocks * inner_rows, width)
    )
    f32, dma = jnp.float32, pltpu.SemaphoreType.DMA
    vmem = pltpu.VMEM
    out = pl.pallas_call(
        body,
        out_shape=pltpu.VMEM((2, groups, 8, width), f32),
        in_specs=[pl.BlockSpec(memory_space=pl.ANY)] * 7,
        out_specs=pl.BlockSpec(memory_space=pltpu.VMEM),
        scratch_shapes=[
            vmem((2, layers, rows + 2 * HALO, columns), f32),
            vmem((layers, rows + 2 * HALO, columns), f32),
            vmem((groups, 8, width), f32),
            vmem((1, count), jnp.int32),
            vmem((1, count), jnp.int32),
            vmem((2 * count, width), f32),
            vmem((count, width), f32),
            vmem((2, layers, rows, columns), f32),
            vmem((groups, 3, 8, width), f32),
            vmem((groups, 2, 8, width), f32),
            vmem((depth + 2, 8, width), f32),
            vmem((groups, 3, 8, width), f32),
            vmem((depth + 2, 8, width), f32),
            vmem((depth, 8, width), f32),
            vmem((depth, 8, width), f32),
            vmem((depth, 8, width), f32),
            dma((7,)),
            dma((2, 2)),
            dma((2, 2)),
            dma(()),
            dma(()),
            dma(()),
            dma(()),
            pltpu.SemaphoreType.REGULAR((2,)),
            pltpu.SemaphoreType.REGULAR,
        ],
        compiler_params=pltpu.CompilerParams(collective_id=0, has_side_effects=True),
        name="relax",
    )(
        in_plane_force,
        stiffness,
        cross,
        patch_dest.reshape(1, count),
        patch_pos.reshape(1, count),
        patch_flow.reshape(2 * count, width),
        patch_conf.reshape(count, width),
    )
    return (
        out.reshape(2, depth, blocks, inner_rows, width)
        .transpose(0, 1, 3, 2, 4)
        .reshape(2, depth, inner_rows, columns)
    )


def solution(mesh):
    placed = (
        P(None, "sec", "tile", None),
        P("sec", "tile", None),
        P(None, ("tile", "sec"), None),
        P("sec", "tile", None, None),
        P("sec", "tile", None),
        P("sec", "tile", None, None, None),
        P("sec", "tile", None, None),
    )
    return jax.shard_map(
        per_device,
        mesh=mesh,
        in_specs=placed,
        out_specs=P(None, None, ("tile", "sec"), None),
        check_vma=False,
    )
```

```python
import functools

import jax
import jax.numpy as jnp
from jax import lax
from jax.experimental import pallas as pl
from jax.experimental.pallas import tpu as pltpu
from jax.sharding import PartitionSpec as P

ISTEPS = 8
ZSTEPS = 8
STEP_PLANE = 0.12
STEP_CROSS = 0.15
LANES = 128
HALO = 8
RUN = 4
CHUNK = 32
DEFER = 24


def plane_steps(force, stiff):
    rows, columns = force.shape[1:]
    drive, pace = STEP_PLANE * force, STEP_PLANE * stiff
    keep = 1.0 - 4.0 * pace
    blocks = [slice(at, at + LANES) for at in range(0, columns, LANES)]
    drive, pace, keep = [[value[..., block] for block in blocks] for value in (drive, pace, keep)]
    lane = lax.broadcasted_iota(jnp.int32, drive[0].shape, 2)
    first, last = lane == 0, lane == LANES - 1
    field = drive
    for _ in range(1, ISTEPS):
        right = [pltpu.roll(value, LANES - 1, 2) for value in field] + [0.0]
        left = [0.0] + [pltpu.roll(value, 1, 2) for value in field]
        stepped = []
        for i, value in enumerate(field):
            beside = jnp.where(first, left[i], left[i + 1]) + jnp.where(last, right[i + 1], right[i])
            around = beside + (pltpu.roll(value, 1, 1) + pltpu.roll(value, rows - 1, 1))
            stepped.append(keep[i] * value + (pace[i] * around + drive[i]))
        field = stepped
    return jnp.concatenate(field, axis=2)


def split3(value):
    high = value.astype(jnp.bfloat16)
    rest = value - high.astype(jnp.float32)
    middle = rest.astype(jnp.bfloat16)
    low = (rest - middle.astype(jnp.float32)).astype(jnp.bfloat16)
    return high, middle, low


def pair_halves(a, b):
    lower = lax.broadcasted_iota(jnp.int32, a.shape, 1) < 4
    return jnp.where(lower, a, pltpu.roll(b, 4, 1)), jnp.where(lower, pltpu.roll(a, 4, 1), b)


def body(
    force_hbm, stiff_hbm, cross_hbm, dest_hbm, pos_hbm, flow_hbm, conf_hbm, out_ref,
    fbuf, sbuf, zbuf, dest, pos, flow, conf, vbuf,
    send_p, send_f, recv_f, recv_p, other, near, far, bend,
    local_sem, halo_send, halo_recv, p_send, p_recv, f_send, f_recv, ready, met,
):
    groups = lax.axis_size("sec")
    tiles = lax.axis_size("tile")
    me = lax.axis_index("sec")
    tile = lax.axis_index("tile")
    rows = force_hbm.shape[2]
    layers = force_hbm.shape[1]
    depth = groups * layers
    mesh = pl.DeviceIdType.MESH

    has_side = (tile > 0, tile < tiles - 1)
    neighbour = (lax.rem(tile + tiles - 1, tiles), lax.rem(tile + 1, tiles))
    greets = (lax.rem(tile, RUN) == 0, lax.rem(tile, RUN) != RUN - 1)

    barrier = pltpu.get_barrier_semaphore()

    core = lax.rem(me, 2)
    partner = me + 1 - 2 * core

    half = groups // 2
    split = lax.rem(tile, RUN) < RUN // 2

    direct = lax.rem(tile, RUN) == RUN // 2

    def in_first(peer):
        return split & (peer > 0) & (peer < half)

    def peer_at(k):
        level = jnp.where(direct, groups // 8 - 1 - k // 8, k // 8)
        return level * 8 + lax.rem(me + k, 8)

    first = in_first(me)

    @pl.when((core == 1) & jnp.logical_not(first))
    def _():
        pl.semaphore_signal(barrier, inc=1, device_id={"sec": partner}, device_id_type=mesh)

    for side in range(2):

        @pl.when(has_side[side] & greets[side])
        def _():
            target = {"sec": me - core, "tile": neighbour[side]}
            pl.semaphore_signal(barrier, inc=1, device_id=target, device_id_type=mesh)

    loads = [
        pltpu.make_async_copy(source, target, local_sem.at[i])
        for i, (source, target) in enumerate(
            (
                (dest_hbm, dest),
                (pos_hbm, pos),
                (conf_hbm, conf),
                (flow_hbm, flow),
                (stiff_hbm, sbuf.at[:, pl.ds(HALO, rows), :]),
                (force_hbm, fbuf.at[:, :, pl.ds(HALO, rows), :]),
                (cross_hbm, zbuf),
            )
        )
    ]
    def halo_copy(index, values, buffer, side):
        lead = (slice(None),) * (len(buffer.shape) - 2)
        reach = ISTEPS - 1 - index
        source, target = ((0, rows + HALO), (rows - reach, HALO - reach))[side]
        return pltpu.make_async_remote_copy(
            src_ref=values.at[lead + (pl.ds(source, reach), slice(None))],
            dst_ref=buffer.at[lead + (pl.ds(target, reach), slice(None))],
            send_sem=halo_send.at[index, side],
            recv_sem=halo_recv.at[index, 1 - side],
            device_id={"tile": neighbour[side]},
            device_id_type=mesh,
        )

    def halo_copies(side):
        return halo_copy(0, force_hbm, fbuf, side), halo_copy(1, stiff_hbm, sbuf, side)

    def meet():
        @pl.when(core == 0)
        def _():
            members = half - 1 - first.astype(jnp.int32)
            waits = jnp.where(split, members, 0) + (partner >= half).astype(jnp.int32)
            waits = jnp.where(split, waits, 1)
            for side in range(2):
                waits = waits + 2 * (has_side[side] & jnp.logical_not(greets[side])).astype(jnp.int32)
            pl.semaphore_wait(barrier, waits)
            pl.semaphore_signal(met, inc=1, device_id={"sec": partner}, device_id_type=mesh)

        @pl.when(core == 1)
        def _():
            pl.semaphore_wait(met, 1)

        for side in range(2):

            @pl.when(has_side[side] & jnp.logical_not(greets[side]))
            def _():
                pl.semaphore_signal(ready.at[1 - side], inc=1, device_id={"tile": neighbour[side]}, device_id_type=mesh)
                for copy in halo_copies(side):
                    copy.start()

    for load in loads:
        load.start()
    pl.when(jnp.logical_not(split))(meet)

    @pl.loop(0, half, unroll=True)
    def _(k):
        collector = 2 * lax.rem(me // 2 + k, half) + 1 - first.astype(jnp.int32)

        @pl.when(collector != me)
        def _():
            pl.semaphore_signal(barrier, inc=1, device_id={"sec": collector}, device_id_type=mesh)

    for load in loads[:6]:
        load.wait()

    count = conf.shape[0]
    place = pos[...]
    slot = dest[...] * 8 + (place // 4) * 4 + (place % 2) * 2 + (place // 2) % 2
    hot = (lax.broadcasted_iota(jnp.int32, (count, count), 0) == slot).astype(jnp.float32).astype(jnp.bfloat16)
    confidence = conf[...]
    payload = jnp.concatenate(
        [confidence * flow[pl.ds(0, count, stride=2), :], confidence * flow[pl.ds(1, count, stride=2), :], confidence],
        axis=1,
    )
    high, middle, low = [jnp.dot(hot, part, preferred_element_type=jnp.float32) for part in split3(payload)]
    grid = high + middle + low
    pull = [grid[:, c * LANES : (c + 1) * LANES].reshape(groups, 8, LANES) for c in range(2)]
    front, back = pair_halves(*pull)
    send_p[:, 0] = front
    send_p[:, 1] = back
    send_p[:, 2] = grid[:, 2 * LANES :].reshape(groups, 8, LANES)

    blank = jnp.zeros((8, LANES), jnp.float32)
    for buffer in (recv_f, other):
        buffer[0] = blank
        buffer[depth + 1] = blank

    pl.when(split)(meet)

    def patch_copy(peer):
        return pltpu.make_async_remote_copy(
            src_ref=send_p.at[peer],
            dst_ref=recv_p.at[me],
            send_sem=p_send,
            recv_sem=p_recv,
            device_id={"sec": peer},
            device_id_type=mesh,
        )

    def field_copy(peer):
        return pltpu.make_async_remote_copy(
            src_ref=send_f.at[peer],
            dst_ref=recv_f.at[pl.ds(1 + 2 * me, 2)],
            send_sem=f_send,
            recv_sem=f_recv,
            device_id={"sec": peer},
            device_id_type=mesh,
        )

    def answer(when):
        for side in (1, 0):

            @pl.when(when & has_side[side] & greets[side])
            def _():
                pl.semaphore_wait(ready.at[side], 1)
                for copy in halo_copies(side):
                    copy.start()

    @pl.when(split)
    def _():
        @pl.loop(0, half)
        def _(k):
            peer = peer_at(k)

            @pl.when(in_first(peer) & (peer != me))
            def _():
                patch_copy(peer).start()

    def pack(rb, layer, blocks):
        for k in range(4):
            pieces = [
                blocks[c][2 * k : 2 * k + 2, xb * LANES : (xb + 1) * LANES] for c in range(2) for xb in range(2)
            ]
            send_f[4 * rb + k, layer] = jnp.concatenate(pieces, axis=0)

    for layer in range(layers):
        vbuf[:, layer] = plane_steps(
            fbuf[:, layer, pl.ds(HALO, rows), :], sbuf[layer, pl.ds(HALO, rows), :][None]
        )

        @pl.loop(1, rows // 8 - 1)
        def _(rb):
            at = pl.ds(pl.multiple_of(rb * 8, 8), 8)
            pack(rb, layer, [vbuf[c, layer, at, :] for c in range(2)])

    @pl.when(core == 1)
    def _():
        others = jnp.where(split, half + 1, groups)
        pl.semaphore_wait(barrier, others - (jnp.logical_not(first)).astype(jnp.int32))
        pl.semaphore_signal(met, inc=1, device_id={"sec": partner}, device_id_type=mesh)

    @pl.when(core == 0)
    def _():
        pl.semaphore_wait(met, 1)

    answer(direct)

    def send_patches(low, high):
        @pl.loop(low, high)
        def _(k):
            peer = peer_at(k)

            @pl.when(jnp.logical_not(in_first(peer)) & (peer != me))
            def _():
                patch_copy(peer).start()

    send_patches(0, DEFER)
    answer(jnp.logical_not(direct))
    send_patches(DEFER, groups)

    def send_inner():
        @pl.loop(0, groups)
        def _(k):
            peer = peer_at(k)
            held = (lax.rem(peer, 8) < 4) == (peer < half)

            @pl.when((peer >= 4) & (peer < groups - 4) & (peer != me) & jnp.logical_not(held))
            def _():
                field_copy(peer).start()

    send_inner()

    def both(halves):
        lower = lax.broadcasted_iota(jnp.int32, halves.shape, 1) < 4
        turned = pltpu.roll(halves, 4, 1)
        return jnp.where(lower, halves, turned), jnp.where(lower, turned, halves)

    loads[6].wait()
    recv_p[me] = send_p[me]

    lead = (lax.rem(tile, RUN) == 0) | (lax.rem(tile, RUN) == RUN - 1)

    @pl.loop(0, 2)
    def _(turn):
        side = jnp.where(lead, turn, 1 - turn)
        inside = jnp.where(side == 0, tile > 0, tile < tiles - 1)
        base = pl.multiple_of(side * (rows - HALO), HALO)

        @pl.when(inside)
        def _():
            for index, buffer in enumerate((fbuf, sbuf)):
                reach = ISTEPS - 1 - index
                block = buffer.at[(slice(None),) * (len(buffer.shape) - 2) + (pl.ds(HALO, reach), slice(None))]
                pltpu.make_async_copy(block, block, halo_recv.at[index, side]).wait()

        for layer in range(layers):
            force = fbuf[:, layer, pl.ds(base, 3 * HALO), :]
            stiff = sbuf[layer, pl.ds(base, 3 * HALO), :][None]
            row = lax.broadcasted_iota(jnp.int32, force.shape, 1)
            edge = jnp.where(side == 0, row, 3 * HALO - 1 - row) < HALO
            empty = edge & jnp.logical_not(inside)
            force = jnp.where(empty, 0.0, force)
            stiff = jnp.where(empty[:1], 0.0, stiff)
            field = plane_steps(force, stiff)
            pack(side * (rows // 8 - 1), layer, [field[c, HALO : 2 * HALO] for c in range(2)])

        for block in (side * (groups - 4), 8 + side * (groups - 20)):

            @pl.loop(0, 4)
            def _(k):
                peer = block + k

                @pl.when(peer != me)
                def _():
                    field_copy(peer).start()


    recv_f[pl.ds(1 + 2 * me, 2)] = send_f[me]

    pltpu.make_async_copy(recv_p.at[pl.ds(1, groups - 1)], recv_p.at[pl.ds(1, groups - 1)], p_recv).wait()

    @pl.loop(0, groups - 1)
    def _(s):
        one, two = pl.ds(2 * s, 1), pl.ds(2 * s + 1, 1)
        k_even, k_odd = both(zbuf[pl.ds(s, 1)])
        w_even, w_odd = both(recv_p[pl.ds(s, 1), 2])
        w_next, _ = both(recv_p[pl.ds(s + 1, 1), 2])
        p_even, p_odd, p_next = recv_p[pl.ds(s, 1), 0], recv_p[pl.ds(s, 1), 1], recv_p[pl.ds(s + 1, 1), 0]
        near[one] = STEP_CROSS * (k_even + w_even)
        near[two] = STEP_CROSS * (k_odd + w_odd)
        far[one] = STEP_CROSS * (k_even + w_odd)
        far[two] = STEP_CROSS * (k_odd + w_next)
        bend[one] = STEP_CROSS * (p_even - p_odd)
        bend[two] = STEP_CROSS * (p_odd - p_next)

    k_even, k_odd = both(zbuf[pl.ds(groups - 1, 1)])
    w_even, w_odd = both(recv_p[pl.ds(groups - 1, 1), 2])
    p_even, p_odd = recv_p[pl.ds(groups - 1, 1), 0], recv_p[pl.ds(groups - 1, 1), 1]
    near[pl.ds(depth - 2, 1)] = STEP_CROSS * (k_even + w_even)
    near[pl.ds(depth - 1, 1)] = STEP_CROSS * (k_odd + w_odd)
    far[pl.ds(depth - 2, 1)] = STEP_CROSS * (k_even + w_odd)
    far[pl.ds(depth - 1, 1)] = STEP_CROSS * k_odd
    bend[pl.ds(depth - 2, 1)] = STEP_CROSS * (p_even - p_odd)
    bend[pl.ds(depth - 1, 1)] = STEP_CROSS * p_odd

    pltpu.make_async_copy(recv_f.at[pl.ds(1, depth - 2)], recv_f.at[pl.ds(1, depth - 2)], f_recv).wait()

    for step in range(ZSTEPS):
        source, target = (recv_f, other) if step % 2 == 0 else (other, recv_f)

        @pl.loop(0, depth // CHUNK)
        def _(i):
            z = pl.multiple_of(i * CHUNK, CHUNK)
            d = source[pl.ds(z, CHUNK + 2)]
            slope = d[1:] - d[:-1]
            at = pl.ds(z, CHUNK)
            d = d[1:-1] + ((far[at] * slope[1:] - near[at] * slope[:-1]) + bend[at])
            if step < ZSTEPS - 1:
                target[pl.ds(z + 1, CHUNK)] = d
            else:
                d = d.reshape(CHUNK // 2, 2, 8, LANES)
                even, odd = pair_halves(d[:, 0], d[:, 1])
                half = pl.ds(pl.multiple_of(i * (CHUNK // 2), CHUNK // 2), CHUNK // 2)
                out_ref[0, half] = even
                out_ref[1, half] = odd

    for side in range(2):

        @pl.when(has_side[side])
        def _():
            for copy in halo_copies(side):
                copy.wait_send()

    pltpu.make_async_copy(send_p.at[pl.ds(1, groups - 1)], send_p.at[pl.ds(1, groups - 1)], p_send).wait()
    pltpu.make_async_copy(send_f.at[pl.ds(1, groups - 1)], send_f.at[pl.ds(1, groups - 1)], f_send).wait()


def per_device(
    in_plane_force, stiffness, stiffness_z, patch_dest, patch_pos, patch_flow, patch_conf
):
    groups = lax.axis_size("sec")
    _, layers, rows, columns = in_plane_force.shape
    inner_rows = rows // groups
    width = patch_flow.shape[-1]
    blocks = columns // width
    count = patch_pos.shape[2]
    depth = layers * groups
    cross = (
        stiffness_z.reshape(depth, inner_rows, blocks, width)
        .transpose(0, 2, 1, 3)
        .reshape(groups, layers * blocks * inner_rows, width)
    )
    f32, dma = jnp.float32, pltpu.SemaphoreType.DMA
    vmem = pltpu.VMEM
    out = pl.pallas_call(
        body,
        out_shape=pltpu.VMEM((2, groups, 8, width), f32),
        in_specs=[pl.BlockSpec(memory_space=pl.ANY)] * 7,
        out_specs=pl.BlockSpec(memory_space=pltpu.VMEM),
        scratch_shapes=[
            vmem((2, layers, rows + 2 * HALO, columns), f32),
            vmem((layers, rows + 2 * HALO, columns), f32),
            vmem((groups, 8, width), f32),
            vmem((1, count), jnp.int32),
            vmem((1, count), jnp.int32),
            vmem((2 * count, width), f32),
            vmem((count, width), f32),
            vmem((2, layers, rows, columns), f32),
            vmem((groups, 3, 8, width), f32),
            vmem((groups, 2, 8, width), f32),
            vmem((depth + 2, 8, width), f32),
            vmem((groups, 3, 8, width), f32),
            vmem((depth + 2, 8, width), f32),
            vmem((depth, 8, width), f32),
            vmem((depth, 8, width), f32),
            vmem((depth, 8, width), f32),
            dma((7,)),
            dma((2, 2)),
            dma((2, 2)),
            dma(()),
            dma(()),
            dma(()),
            dma(()),
            pltpu.SemaphoreType.REGULAR((2,)),
            pltpu.SemaphoreType.REGULAR,
        ],
        compiler_params=pltpu.CompilerParams(collective_id=0, has_side_effects=True),
        name="relax",
    )(
        in_plane_force,
        stiffness,
        cross,
        patch_dest.reshape(1, count),
        patch_pos.reshape(1, count),
        patch_flow.reshape(2 * count, width),
        patch_conf.reshape(count, width),
    )
    return (
        out.reshape(2, depth, blocks, inner_rows, width)
        .transpose(0, 1, 3, 2, 4)
        .reshape(2, depth, inner_rows, columns)
    )


def solution(mesh):
    placed = (
        P(None, "sec", "tile", None),
        P("sec", "tile", None),
        P(None, ("tile", "sec"), None),
        P("sec", "tile", None, None),
        P("sec", "tile", None),
        P("sec", "tile", None, None, None),
        P("sec", "tile", None, None),
    )
    return jax.shard_map(
        per_device,
        mesh=mesh,
        in_specs=placed,
        out_specs=P(None, None, ("tile", "sec"), None),
        check_vma=False,
    )
```

```python
import functools

import jax
import jax.numpy as jnp
from jax import lax
from jax.experimental import pallas as pl
from jax.experimental.pallas import tpu as pltpu
from jax.sharding import PartitionSpec as P

ISTEPS = 8
ZSTEPS = 8
STEP_PLANE = 0.12
STEP_CROSS = 0.15
LANES = 128
HALO = 8
RUN = 4
CHUNK = 32
DEFER = 24


def plane_steps(force, stiff):
    rows, columns = force.shape[1:]
    drive, pace = STEP_PLANE * force, STEP_PLANE * stiff
    keep = 1.0 - 4.0 * pace
    blocks = [slice(at, at + LANES) for at in range(0, columns, LANES)]
    drive, pace, keep = [[value[..., block] for block in blocks] for value in (drive, pace, keep)]
    lane = lax.broadcasted_iota(jnp.int32, drive[0].shape, 2)
    first, last = lane == 0, lane == LANES - 1
    field = drive
    for _ in range(1, ISTEPS):
        right = [pltpu.roll(value, LANES - 1, 2) for value in field] + [0.0]
        left = [0.0] + [pltpu.roll(value, 1, 2) for value in field]
        stepped = []
        for i, value in enumerate(field):
            beside = jnp.where(first, left[i], left[i + 1]) + jnp.where(last, right[i + 1], right[i])
            around = beside + (pltpu.roll(value, 1, 1) + pltpu.roll(value, rows - 1, 1))
            stepped.append(keep[i] * value + (pace[i] * around + drive[i]))
        field = stepped
    return jnp.concatenate(field, axis=2)


def split3(value):
    high = value.astype(jnp.bfloat16)
    rest = value - high.astype(jnp.float32)
    middle = rest.astype(jnp.bfloat16)
    low = (rest - middle.astype(jnp.float32)).astype(jnp.bfloat16)
    return high, middle, low


def pair_halves(a, b):
    lower = lax.broadcasted_iota(jnp.int32, a.shape, 1) < 4
    return jnp.where(lower, a, pltpu.roll(b, 4, 1)), jnp.where(lower, pltpu.roll(a, 4, 1), b)


def body(
    force_hbm, stiff_hbm, cross_hbm, dest_hbm, pos_hbm, flow_hbm, conf_hbm, out_ref,
    fbuf, sbuf, zbuf, dest, pos, flow, conf, vbuf,
    send_p, send_f, recv_f, recv_p, other, near, far, bend,
    local_sem, halo_send, halo_recv, p_send, p_recv, f_send, f_recv, ready, met,
):
    groups = lax.axis_size("sec")
    tiles = lax.axis_size("tile")
    me = lax.axis_index("sec")
    tile = lax.axis_index("tile")
    rows = force_hbm.shape[2]
    layers = force_hbm.shape[1]
    depth = groups * layers
    mesh = pl.DeviceIdType.MESH

    has_side = (tile > 0, tile < tiles - 1)
    neighbour = (lax.rem(tile + tiles - 1, tiles), lax.rem(tile + 1, tiles))
    greets = (lax.rem(tile, RUN) == 0, lax.rem(tile, RUN) != RUN - 1)

    barrier = pltpu.get_barrier_semaphore()

    core = lax.rem(me, 2)
    partner = me + 1 - 2 * core

    half = groups // 2
    split = lax.rem(tile, RUN) < RUN // 2

    direct = lax.rem(tile, RUN) == RUN // 2

    def in_first(peer):
        return split & (peer > 0) & (peer < half)

    def peer_at(k):
        level = jnp.where(direct, groups // 8 - 1 - k // 8, k // 8)
        return level * 8 + lax.rem(me + k, 8)

    first = in_first(me)

    @pl.when((core == 1) & jnp.logical_not(first))
    def _():
        pl.semaphore_signal(barrier, inc=1, device_id={"sec": partner}, device_id_type=mesh)

    for side in range(2):

        @pl.when(has_side[side] & greets[side])
        def _():
            target = {"sec": me - core, "tile": neighbour[side]}
            pl.semaphore_signal(barrier, inc=1, device_id=target, device_id_type=mesh)

    loads = [
        pltpu.make_async_copy(source, target, local_sem.at[i])
        for i, (source, target) in enumerate(
            (
                (dest_hbm, dest),
                (pos_hbm, pos),
                (conf_hbm, conf),
                (flow_hbm, flow),
                (stiff_hbm, sbuf.at[:, pl.ds(HALO, rows), :]),
                (force_hbm, fbuf.at[:, :, pl.ds(HALO, rows), :]),
                (cross_hbm, zbuf),
            )
        )
    ]
    def halo_copy(index, values, buffer, side):
        lead = (slice(None),) * (len(buffer.shape) - 2)
        reach = ISTEPS - 1 - index
        source, target = ((0, rows + HALO), (rows - reach, HALO - reach))[side]
        return pltpu.make_async_remote_copy(
            src_ref=values.at[lead + (pl.ds(source, reach), slice(None))],
            dst_ref=buffer.at[lead + (pl.ds(target, reach), slice(None))],
            send_sem=halo_send.at[index, side],
            recv_sem=halo_recv.at[index, 1 - side],
            device_id={"tile": neighbour[side]},
            device_id_type=mesh,
        )

    def halo_copies(side):
        return halo_copy(0, force_hbm, fbuf, side), halo_copy(1, stiff_hbm, sbuf, side)

    def meet():
        @pl.when(core == 0)
        def _():
            members = half - 1 - first.astype(jnp.int32)
            waits = jnp.where(split, members, 0) + (partner >= half).astype(jnp.int32)
            waits = jnp.where(split, waits, 1)
            for side in range(2):
                waits = waits + 2 * (has_side[side] & jnp.logical_not(greets[side])).astype(jnp.int32)
            pl.semaphore_wait(barrier, waits)
            pl.semaphore_signal(met, inc=1, device_id={"sec": partner}, device_id_type=mesh)

        @pl.when(core == 1)
        def _():
            pl.semaphore_wait(met, 1)

        for side in range(2):

            @pl.when(has_side[side] & jnp.logical_not(greets[side]))
            def _():
                pl.semaphore_signal(ready.at[1 - side], inc=1, device_id={"tile": neighbour[side]}, device_id_type=mesh)
                for copy in halo_copies(side):
                    copy.start()

    for load in loads:
        load.start()
    pl.when(jnp.logical_not(split))(meet)

    @pl.loop(0, half, unroll=True)
    def _(k):
        collector = 2 * lax.rem(me // 2 + k, half) + 1 - first.astype(jnp.int32)

        @pl.when(collector != me)
        def _():
            pl.semaphore_signal(barrier, inc=1, device_id={"sec": collector}, device_id_type=mesh)

    for load in loads[:6]:
        load.wait()

    count = conf.shape[0]
    place = pos[...]
    slot = dest[...] * 8 + (place // 4) * 4 + (place % 2) * 2 + (place // 2) % 2
    hot = (lax.broadcasted_iota(jnp.int32, (count, count), 0) == slot).astype(jnp.float32).astype(jnp.bfloat16)
    confidence = conf[...]
    payload = jnp.concatenate(
        [confidence * flow[pl.ds(0, count, stride=2), :], confidence * flow[pl.ds(1, count, stride=2), :], confidence],
        axis=1,
    )
    high, middle, low = [jnp.dot(hot, part, preferred_element_type=jnp.float32) for part in split3(payload)]
    grid = high + middle + low
    pull = [grid[:, c * LANES : (c + 1) * LANES].reshape(groups, 8, LANES) for c in range(2)]
    front, back = pair_halves(*pull)
    send_p[:, 0] = front
    send_p[:, 1] = back
    send_p[:, 2] = grid[:, 2 * LANES :].reshape(groups, 8, LANES)

    blank = jnp.zeros((8, LANES), jnp.float32)
    for buffer in (recv_f, other):
        buffer[0] = blank
        buffer[depth + 1] = blank

    pl.when(split)(meet)

    def patch_copy(peer):
        return pltpu.make_async_remote_copy(
            src_ref=send_p.at[peer],
            dst_ref=recv_p.at[me],
            send_sem=p_send,
            recv_sem=p_recv,
            device_id={"sec": peer},
            device_id_type=mesh,
        )

    def field_copy(peer):
        return pltpu.make_async_remote_copy(
            src_ref=send_f.at[peer],
            dst_ref=recv_f.at[pl.ds(1 + 2 * me, 2)],
            send_sem=f_send,
            recv_sem=f_recv,
            device_id={"sec": peer},
            device_id_type=mesh,
        )

    def answer(when):
        for side in (1, 0):

            @pl.when(when & has_side[side] & greets[side])
            def _():
                pl.semaphore_wait(ready.at[side], 1)
                for copy in halo_copies(side):
                    copy.start()

    @pl.when(split)
    def _():
        @pl.loop(0, half, unroll=4)
        def _(k):
            peer = peer_at(k)

            @pl.when(in_first(peer) & (peer != me))
            def _():
                patch_copy(peer).start()

    def pack(rb, layer, blocks):
        for k in range(4):
            pieces = [
                blocks[c][2 * k : 2 * k + 2, xb * LANES : (xb + 1) * LANES] for c in range(2) for xb in range(2)
            ]
            send_f[4 * rb + k, layer] = jnp.concatenate(pieces, axis=0)

    for layer in range(layers):
        vbuf[:, layer] = plane_steps(
            fbuf[:, layer, pl.ds(HALO, rows), :], sbuf[layer, pl.ds(HALO, rows), :][None]
        )

        @pl.loop(1, rows // 8 - 1)
        def _(rb):
            at = pl.ds(pl.multiple_of(rb * 8, 8), 8)
            pack(rb, layer, [vbuf[c, layer, at, :] for c in range(2)])

    @pl.when(core == 1)
    def _():
        others = jnp.where(split, half + 1, groups)
        pl.semaphore_wait(barrier, others - (jnp.logical_not(first)).astype(jnp.int32))
        pl.semaphore_signal(met, inc=1, device_id={"sec": partner}, device_id_type=mesh)

    @pl.when(core == 0)
    def _():
        pl.semaphore_wait(met, 1)

    answer(direct)

    def send_patches(low, high):
        @pl.loop(low, high, unroll=4)
        def _(k):
            peer = peer_at(k)

            @pl.when(jnp.logical_not(in_first(peer)) & (peer != me))
            def _():
                patch_copy(peer).start()

    send_patches(0, DEFER)
    answer(jnp.logical_not(direct))
    send_patches(DEFER, groups)

    def send_inner():
        @pl.loop(0, groups, unroll=4)
        def _(k):
            peer = peer_at(k)
            held = (lax.rem(peer, 8) < 4) == (peer < half)

            @pl.when((peer >= 4) & (peer < groups - 4) & (peer != me) & jnp.logical_not(held))
            def _():
                field_copy(peer).start()

    send_inner()

    def both(halves):
        lower = lax.broadcasted_iota(jnp.int32, halves.shape, 1) < 4
        turned = pltpu.roll(halves, 4, 1)
        return jnp.where(lower, halves, turned), jnp.where(lower, turned, halves)

    loads[6].wait()
    recv_p[me] = send_p[me]

    lead = (lax.rem(tile, RUN) == 0) | (lax.rem(tile, RUN) == RUN - 1)

    @pl.loop(0, 2)
    def _(turn):
        side = jnp.where(lead, turn, 1 - turn)
        inside = jnp.where(side == 0, tile > 0, tile < tiles - 1)
        base = pl.multiple_of(side * (rows - HALO), HALO)

        @pl.when(inside)
        def _():
            for index, buffer in enumerate((fbuf, sbuf)):
                reach = ISTEPS - 1 - index
                block = buffer.at[(slice(None),) * (len(buffer.shape) - 2) + (pl.ds(HALO, reach), slice(None))]
                pltpu.make_async_copy(block, block, halo_recv.at[index, side]).wait()

        for layer in range(layers):
            force = fbuf[:, layer, pl.ds(base, 3 * HALO), :]
            stiff = sbuf[layer, pl.ds(base, 3 * HALO), :][None]
            row = lax.broadcasted_iota(jnp.int32, force.shape, 1)
            edge = jnp.where(side == 0, row, 3 * HALO - 1 - row) < HALO
            empty = edge & jnp.logical_not(inside)
            force = jnp.where(empty, 0.0, force)
            stiff = jnp.where(empty[:1], 0.0, stiff)
            field = plane_steps(force, stiff)
            pack(side * (rows // 8 - 1), layer, [field[c, HALO : 2 * HALO] for c in range(2)])

        for block in (side * (groups - 4), 8 + side * (groups - 20)):

            @pl.loop(0, 4)
            def _(k):
                peer = block + k

                @pl.when(peer != me)
                def _():
                    field_copy(peer).start()


    recv_f[pl.ds(1 + 2 * me, 2)] = send_f[me]

    pltpu.make_async_copy(recv_p.at[pl.ds(1, groups - 1)], recv_p.at[pl.ds(1, groups - 1)], p_recv).wait()

    @pl.loop(0, groups - 1)
    def _(s):
        one, two = pl.ds(2 * s, 1), pl.ds(2 * s + 1, 1)
        k_even, k_odd = both(zbuf[pl.ds(s, 1)])
        w_even, w_odd = both(recv_p[pl.ds(s, 1), 2])
        w_next, _ = both(recv_p[pl.ds(s + 1, 1), 2])
        p_even, p_odd, p_next = recv_p[pl.ds(s, 1), 0], recv_p[pl.ds(s, 1), 1], recv_p[pl.ds(s + 1, 1), 0]
        near[one] = STEP_CROSS * (k_even + w_even)
        near[two] = STEP_CROSS * (k_odd + w_odd)
        far[one] = STEP_CROSS * (k_even + w_odd)
        far[two] = STEP_CROSS * (k_odd + w_next)
        bend[one] = STEP_CROSS * (p_even - p_odd)
        bend[two] = STEP_CROSS * (p_odd - p_next)

    k_even, k_odd = both(zbuf[pl.ds(groups - 1, 1)])
    w_even, w_odd = both(recv_p[pl.ds(groups - 1, 1), 2])
    p_even, p_odd = recv_p[pl.ds(groups - 1, 1), 0], recv_p[pl.ds(groups - 1, 1), 1]
    near[pl.ds(depth - 2, 1)] = STEP_CROSS * (k_even + w_even)
    near[pl.ds(depth - 1, 1)] = STEP_CROSS * (k_odd + w_odd)
    far[pl.ds(depth - 2, 1)] = STEP_CROSS * (k_even + w_odd)
    far[pl.ds(depth - 1, 1)] = STEP_CROSS * k_odd
    bend[pl.ds(depth - 2, 1)] = STEP_CROSS * (p_even - p_odd)
    bend[pl.ds(depth - 1, 1)] = STEP_CROSS * p_odd

    pltpu.make_async_copy(recv_f.at[pl.ds(1, depth - 2)], recv_f.at[pl.ds(1, depth - 2)], f_recv).wait()

    for step in range(ZSTEPS):
        source, target = (recv_f, other) if step % 2 == 0 else (other, recv_f)

        @pl.loop(0, depth // CHUNK)
        def _(i):
            z = pl.multiple_of(i * CHUNK, CHUNK)
            d = source[pl.ds(z, CHUNK + 2)]
            slope = d[1:] - d[:-1]
            at = pl.ds(z, CHUNK)
            d = d[1:-1] + ((far[at] * slope[1:] - near[at] * slope[:-1]) + bend[at])
            if step < ZSTEPS - 1:
                target[pl.ds(z + 1, CHUNK)] = d
            else:
                d = d.reshape(CHUNK // 2, 2, 8, LANES)
                even, odd = pair_halves(d[:, 0], d[:, 1])
                half = pl.ds(pl.multiple_of(i * (CHUNK // 2), CHUNK // 2), CHUNK // 2)
                out_ref[0, half] = even
                out_ref[1, half] = odd

    for side in range(2):

        @pl.when(has_side[side])
        def _():
            for copy in halo_copies(side):
                copy.wait_send()

    pltpu.make_async_copy(send_p.at[pl.ds(1, groups - 1)], send_p.at[pl.ds(1, groups - 1)], p_send).wait()
    pltpu.make_async_copy(send_f.at[pl.ds(1, groups - 1)], send_f.at[pl.ds(1, groups - 1)], f_send).wait()


def per_device(
    in_plane_force, stiffness, stiffness_z, patch_dest, patch_pos, patch_flow, patch_conf
):
    groups = lax.axis_size("sec")
    _, layers, rows, columns = in_plane_force.shape
    inner_rows = rows // groups
    width = patch_flow.shape[-1]
    blocks = columns // width
    count = patch_pos.shape[2]
    depth = layers * groups
    cross = (
        stiffness_z.reshape(depth, inner_rows, blocks, width)
        .transpose(0, 2, 1, 3)
        .reshape(groups, layers * blocks * inner_rows, width)
    )
    f32, dma = jnp.float32, pltpu.SemaphoreType.DMA
    vmem = pltpu.VMEM
    out = pl.pallas_call(
        body,
        out_shape=pltpu.VMEM((2, groups, 8, width), f32),
        in_specs=[pl.BlockSpec(memory_space=pl.ANY)] * 7,
        out_specs=pl.BlockSpec(memory_space=pltpu.VMEM),
        scratch_shapes=[
            vmem((2, layers, rows + 2 * HALO, columns), f32),
            vmem((layers, rows + 2 * HALO, columns), f32),
            vmem((groups, 8, width), f32),
            vmem((1, count), jnp.int32),
            vmem((1, count), jnp.int32),
            vmem((2 * count, width), f32),
            vmem((count, width), f32),
            vmem((2, layers, rows, columns), f32),
            vmem((groups, 3, 8, width), f32),
            vmem((groups, 2, 8, width), f32),
            vmem((depth + 2, 8, width), f32),
            vmem((groups, 3, 8, width), f32),
            vmem((depth + 2, 8, width), f32),
            vmem((depth, 8, width), f32),
            vmem((depth, 8, width), f32),
            vmem((depth, 8, width), f32),
            dma((7,)),
            dma((2, 2)),
            dma((2, 2)),
            dma(()),
            dma(()),
            dma(()),
            dma(()),
            pltpu.SemaphoreType.REGULAR((2,)),
            pltpu.SemaphoreType.REGULAR,
        ],
        compiler_params=pltpu.CompilerParams(collective_id=0, has_side_effects=True),
        name="relax",
    )(
        in_plane_force,
        stiffness,
        cross,
        patch_dest.reshape(1, count),
        patch_pos.reshape(1, count),
        patch_flow.reshape(2 * count, width),
        patch_conf.reshape(count, width),
    )
    return (
        out.reshape(2, depth, blocks, inner_rows, width)
        .transpose(0, 1, 3, 2, 4)
        .reshape(2, depth, inner_rows, columns)
    )


def solution(mesh):
    placed = (
        P(None, "sec", "tile", None),
        P("sec", "tile", None),
        P(None, ("tile", "sec"), None),
        P("sec", "tile", None, None),
        P("sec", "tile", None),
        P("sec", "tile", None, None, None),
        P("sec", "tile", None, None),
    )
    return jax.shard_map(
        per_device,
        mesh=mesh,
        in_specs=placed,
        out_specs=P(None, None, ("tile", "sec"), None),
        check_vma=False,
    )
```

```python
import functools

import jax
import jax.numpy as jnp
from jax import lax
from jax.experimental import pallas as pl
from jax.experimental.pallas import tpu as pltpu
from jax.sharding import PartitionSpec as P

ISTEPS = 8
ZSTEPS = 8
STEP_PLANE = 0.12
STEP_CROSS = 0.15
LANES = 128
HALO = 8
RUN = 4
CHUNK = 32
DEFER = 24


def plane_steps(force, stiff):
    rows, columns = force.shape[1:]
    drive, pace = STEP_PLANE * force, STEP_PLANE * stiff
    keep = 1.0 - 4.0 * pace
    blocks = [slice(at, at + LANES) for at in range(0, columns, LANES)]
    drive, pace, keep = [[value[..., block] for block in blocks] for value in (drive, pace, keep)]
    lane = lax.broadcasted_iota(jnp.int32, drive[0].shape, 2)
    first, last = lane == 0, lane == LANES - 1
    field = drive
    for _ in range(1, ISTEPS):
        right = [pltpu.roll(value, LANES - 1, 2) for value in field] + [0.0]
        left = [0.0] + [pltpu.roll(value, 1, 2) for value in field]
        stepped = []
        for i, value in enumerate(field):
            beside = jnp.where(first, left[i], left[i + 1]) + jnp.where(last, right[i + 1], right[i])
            around = beside + (pltpu.roll(value, 1, 1) + pltpu.roll(value, rows - 1, 1))
            stepped.append(keep[i] * value + (pace[i] * around + drive[i]))
        field = stepped
    return jnp.concatenate(field, axis=2)


def split3(value):
    high = value.astype(jnp.bfloat16)
    rest = value - high.astype(jnp.float32)
    middle = rest.astype(jnp.bfloat16)
    low = (rest - middle.astype(jnp.float32)).astype(jnp.bfloat16)
    return high, middle, low


def pair_halves(a, b):
    lower = lax.broadcasted_iota(jnp.int32, a.shape, 1) < 4
    return jnp.where(lower, a, pltpu.roll(b, 4, 1)), jnp.where(lower, pltpu.roll(a, 4, 1), b)


def body(
    force_hbm, stiff_hbm, cross_hbm, dest_hbm, pos_hbm, flow_hbm, conf_hbm, out_ref,
    fbuf, sbuf, zbuf, dest, pos, flow, conf, vbuf,
    send_p, send_f, recv_f, recv_p, other, near, far, bend,
    local_sem, halo_send, halo_recv, p_send, p_recv, f_send, f_recv, ready, met,
):
    groups = lax.axis_size("sec")
    tiles = lax.axis_size("tile")
    me = lax.axis_index("sec")
    tile = lax.axis_index("tile")
    rows = force_hbm.shape[2]
    layers = force_hbm.shape[1]
    depth = groups * layers
    mesh = pl.DeviceIdType.MESH

    has_side = (tile > 0, tile < tiles - 1)
    neighbour = (lax.rem(tile + tiles - 1, tiles), lax.rem(tile + 1, tiles))
    greets = (lax.rem(tile, RUN) == 0, lax.rem(tile, RUN) != RUN - 1)

    barrier = pltpu.get_barrier_semaphore()

    core = lax.rem(me, 2)
    partner = me + 1 - 2 * core

    half = groups // 2
    split = lax.rem(tile, RUN) < RUN // 2

    direct = lax.rem(tile, RUN) == RUN // 2

    def in_first(peer):
        return split & (peer > 0) & (peer < half)

    def peer_at(k):
        level = jnp.where(direct, groups // 8 - 1 - k // 8, k // 8)
        return level * 8 + lax.rem(me + k, 8)

    first = in_first(me)

    @pl.when((core == 1) & jnp.logical_not(first))
    def _():
        pl.semaphore_signal(barrier, inc=1, device_id={"sec": partner}, device_id_type=mesh)

    for side in range(2):

        @pl.when(has_side[side] & greets[side])
        def _():
            target = {"sec": me - core, "tile": neighbour[side]}
            pl.semaphore_signal(barrier, inc=1, device_id=target, device_id_type=mesh)

    loads = [
        pltpu.make_async_copy(source, target, local_sem.at[i])
        for i, (source, target) in enumerate(
            (
                (dest_hbm, dest),
                (pos_hbm, pos),
                (conf_hbm, conf),
                (flow_hbm, flow),
                (stiff_hbm, sbuf.at[:, pl.ds(HALO, rows), :]),
                (force_hbm, fbuf.at[:, :, pl.ds(HALO, rows), :]),
                (cross_hbm, zbuf),
            )
        )
    ]
    def halo_copy(index, values, buffer, side):
        lead = (slice(None),) * (len(buffer.shape) - 2)
        reach = ISTEPS - 1 - index
        source, target = ((0, rows + HALO), (rows - reach, HALO - reach))[side]
        return pltpu.make_async_remote_copy(
            src_ref=values.at[lead + (pl.ds(source, reach), slice(None))],
            dst_ref=buffer.at[lead + (pl.ds(target, reach), slice(None))],
            send_sem=halo_send.at[index, side],
            recv_sem=halo_recv.at[index, 1 - side],
            device_id={"tile": neighbour[side]},
            device_id_type=mesh,
        )

    def halo_copies(side):
        return halo_copy(0, force_hbm, fbuf, side), halo_copy(1, stiff_hbm, sbuf, side)

    def meet():
        @pl.when(core == 0)
        def _():
            members = half - 1 - first.astype(jnp.int32)
            waits = jnp.where(split, members, 0) + (partner >= half).astype(jnp.int32)
            waits = jnp.where(split, waits, 1)
            for side in range(2):
                waits = waits + 2 * (has_side[side] & jnp.logical_not(greets[side])).astype(jnp.int32)
            pl.semaphore_wait(barrier, waits)
            pl.semaphore_signal(met, inc=1, device_id={"sec": partner}, device_id_type=mesh)

        @pl.when(core == 1)
        def _():
            pl.semaphore_wait(met, 1)

        for side in range(2):

            @pl.when(has_side[side] & jnp.logical_not(greets[side]))
            def _():
                pl.semaphore_signal(ready.at[1 - side], inc=1, device_id={"tile": neighbour[side]}, device_id_type=mesh)
                for copy in halo_copies(side):
                    copy.start()

    for load in loads:
        load.start()
    pl.when(jnp.logical_not(split))(meet)

    @pl.loop(0, half, unroll=True)
    def _(k):
        collector = 2 * lax.rem(me // 2 + k, half) + 1 - first.astype(jnp.int32)

        @pl.when(collector != me)
        def _():
            pl.semaphore_signal(barrier, inc=1, device_id={"sec": collector}, device_id_type=mesh)

    for load in loads[:6]:
        load.wait()

    count = conf.shape[0]
    place = pos[...]
    slot = dest[...] * 8 + (place // 4) * 4 + (place % 2) * 2 + (place // 2) % 2
    hot = (lax.broadcasted_iota(jnp.int32, (count, count), 0) == slot).astype(jnp.float32).astype(jnp.bfloat16)
    confidence = conf[...]
    payload = jnp.concatenate(
        [confidence * flow[pl.ds(0, count, stride=2), :], confidence * flow[pl.ds(1, count, stride=2), :], confidence],
        axis=1,
    )
    high, middle, low = [jnp.dot(hot, part, preferred_element_type=jnp.float32) for part in split3(payload)]
    grid = high + middle + low
    pull = [grid[:, c * LANES : (c + 1) * LANES].reshape(groups, 8, LANES) for c in range(2)]
    front, back = pair_halves(*pull)
    send_p[:, 0] = front
    send_p[:, 1] = back
    send_p[:, 2] = grid[:, 2 * LANES :].reshape(groups, 8, LANES)

    blank = jnp.zeros((8, LANES), jnp.float32)
    for buffer in (recv_f, other):
        buffer[0] = blank
        buffer[depth + 1] = blank

    pl.when(split)(meet)

    def patch_copy(peer):
        return pltpu.make_async_remote_copy(
            src_ref=send_p.at[peer],
            dst_ref=recv_p.at[me],
            send_sem=p_send,
            recv_sem=p_recv,
            device_id={"sec": peer},
            device_id_type=mesh,
        )

    def field_copy(peer):
        return pltpu.make_async_remote_copy(
            src_ref=send_f.at[peer],
            dst_ref=recv_f.at[pl.ds(1 + 2 * me, 2)],
            send_sem=f_send,
            recv_sem=f_recv,
            device_id={"sec": peer},
            device_id_type=mesh,
        )

    def answer(when):
        for side in (1, 0):

            @pl.when(when & has_side[side] & greets[side])
            def _():
                pl.semaphore_wait(ready.at[side], 1)
                for copy in halo_copies(side):
                    copy.start()

    @pl.when(split)
    def _():
        @pl.loop(0, half, unroll=4)
        def _(k):
            peer = peer_at(k)

            @pl.when(in_first(peer) & (peer != me))
            def _():
                patch_copy(peer).start()

    def pack(rb, layer, blocks):
        for k in range(4):
            pieces = [
                blocks[c][2 * k : 2 * k + 2, xb * LANES : (xb + 1) * LANES] for c in range(2) for xb in range(2)
            ]
            send_f[4 * rb + k, layer] = jnp.concatenate(pieces, axis=0)

    for layer in range(layers):
        vbuf[:, layer] = plane_steps(
            fbuf[:, layer, pl.ds(HALO, rows), :], sbuf[layer, pl.ds(HALO, rows), :][None]
        )

        @pl.loop(1, rows // 8 - 1)
        def _(rb):
            at = pl.ds(pl.multiple_of(rb * 8, 8), 8)
            pack(rb, layer, [vbuf[c, layer, at, :] for c in range(2)])

    @pl.when(core == 1)
    def _():
        others = jnp.where(split, half + 1, groups)
        pl.semaphore_wait(barrier, others - (jnp.logical_not(first)).astype(jnp.int32))
        pl.semaphore_signal(met, inc=1, device_id={"sec": partner}, device_id_type=mesh)

    @pl.when(core == 0)
    def _():
        pl.semaphore_wait(met, 1)

    answer(direct)

    def send_patches(low, high):
        @pl.loop(low, high, unroll=4)
        def _(k):
            peer = peer_at(k)

            @pl.when(jnp.logical_not(in_first(peer)) & (peer != me))
            def _():
                patch_copy(peer).start()

    send_patches(0, DEFER)
    answer(jnp.logical_not(direct))
    send_patches(DEFER, groups)

    def send_inner():
        @pl.loop(0, groups, unroll=4)
        def _(k):
            peer = peer_at(k)
            held = (lax.rem(peer, 8) < 4) == (peer < half)

            @pl.when((peer >= 4) & (peer < groups - 4) & (peer != me) & jnp.logical_not(held))
            def _():
                field_copy(peer).start()

    send_inner()

    def both(halves):
        lower = lax.broadcasted_iota(jnp.int32, halves.shape, 1) < 4
        turned = pltpu.roll(halves, 4, 1)
        return jnp.where(lower, halves, turned), jnp.where(lower, turned, halves)

    loads[6].wait()
    recv_p[me] = send_p[me]

    lead = (lax.rem(tile, RUN) == 0) | (lax.rem(tile, RUN) == RUN - 1)

    @pl.loop(0, 2)
    def _(turn):
        side = jnp.where(lead, turn, 1 - turn)
        inside = jnp.where(side == 0, tile > 0, tile < tiles - 1)
        base = pl.multiple_of(side * (rows - HALO), HALO)

        @pl.when(inside)
        def _():
            for index, buffer in enumerate((fbuf, sbuf)):
                reach = ISTEPS - 1 - index
                block = buffer.at[(slice(None),) * (len(buffer.shape) - 2) + (pl.ds(HALO, reach), slice(None))]
                pltpu.make_async_copy(block, block, halo_recv.at[index, side]).wait()

        for layer in range(layers):
            force = fbuf[:, layer, pl.ds(base, 3 * HALO), :]
            stiff = sbuf[layer, pl.ds(base, 3 * HALO), :][None]
            row = lax.broadcasted_iota(jnp.int32, force.shape, 1)
            edge = jnp.where(side == 0, row, 3 * HALO - 1 - row) < HALO
            empty = edge & jnp.logical_not(inside)
            force = jnp.where(empty, 0.0, force)
            stiff = jnp.where(empty[:1], 0.0, stiff)
            field = plane_steps(force, stiff)
            pack(side * (rows // 8 - 1), layer, [field[c, HALO : 2 * HALO] for c in range(2)])

        for block in (side * (groups - 4), 8 + side * (groups - 20)):

            @pl.loop(0, 4, unroll=True)
            def _(k):
                peer = block + k

                @pl.when(peer != me)
                def _():
                    field_copy(peer).start()


    recv_f[pl.ds(1 + 2 * me, 2)] = send_f[me]

    pltpu.make_async_copy(recv_p.at[pl.ds(1, groups - 1)], recv_p.at[pl.ds(1, groups - 1)], p_recv).wait()

    @pl.loop(0, groups - 1)
    def _(s):
        one, two = pl.ds(2 * s, 1), pl.ds(2 * s + 1, 1)
        k_even, k_odd = both(zbuf[pl.ds(s, 1)])
        w_even, w_odd = both(recv_p[pl.ds(s, 1), 2])
        w_next, _ = both(recv_p[pl.ds(s + 1, 1), 2])
        p_even, p_odd, p_next = recv_p[pl.ds(s, 1), 0], recv_p[pl.ds(s, 1), 1], recv_p[pl.ds(s + 1, 1), 0]
        near[one] = STEP_CROSS * (k_even + w_even)
        near[two] = STEP_CROSS * (k_odd + w_odd)
        far[one] = STEP_CROSS * (k_even + w_odd)
        far[two] = STEP_CROSS * (k_odd + w_next)
        bend[one] = STEP_CROSS * (p_even - p_odd)
        bend[two] = STEP_CROSS * (p_odd - p_next)

    k_even, k_odd = both(zbuf[pl.ds(groups - 1, 1)])
    w_even, w_odd = both(recv_p[pl.ds(groups - 1, 1), 2])
    p_even, p_odd = recv_p[pl.ds(groups - 1, 1), 0], recv_p[pl.ds(groups - 1, 1), 1]
    near[pl.ds(depth - 2, 1)] = STEP_CROSS * (k_even + w_even)
    near[pl.ds(depth - 1, 1)] = STEP_CROSS * (k_odd + w_odd)
    far[pl.ds(depth - 2, 1)] = STEP_CROSS * (k_even + w_odd)
    far[pl.ds(depth - 1, 1)] = STEP_CROSS * k_odd
    bend[pl.ds(depth - 2, 1)] = STEP_CROSS * (p_even - p_odd)
    bend[pl.ds(depth - 1, 1)] = STEP_CROSS * p_odd

    pltpu.make_async_copy(recv_f.at[pl.ds(1, depth - 2)], recv_f.at[pl.ds(1, depth - 2)], f_recv).wait()

    for step in range(ZSTEPS):
        source, target = (recv_f, other) if step % 2 == 0 else (other, recv_f)

        @pl.loop(0, depth // CHUNK)
        def _(i):
            z = pl.multiple_of(i * CHUNK, CHUNK)
            d = source[pl.ds(z, CHUNK + 2)]
            slope = d[1:] - d[:-1]
            at = pl.ds(z, CHUNK)
            d = d[1:-1] + ((far[at] * slope[1:] - near[at] * slope[:-1]) + bend[at])
            if step < ZSTEPS - 1:
                target[pl.ds(z + 1, CHUNK)] = d
            else:
                d = d.reshape(CHUNK // 2, 2, 8, LANES)
                even, odd = pair_halves(d[:, 0], d[:, 1])
                half = pl.ds(pl.multiple_of(i * (CHUNK // 2), CHUNK // 2), CHUNK // 2)
                out_ref[0, half] = even
                out_ref[1, half] = odd

    for side in range(2):

        @pl.when(has_side[side])
        def _():
            for copy in halo_copies(side):
                copy.wait_send()

    pltpu.make_async_copy(send_p.at[pl.ds(1, groups - 1)], send_p.at[pl.ds(1, groups - 1)], p_send).wait()
    pltpu.make_async_copy(send_f.at[pl.ds(1, groups - 1)], send_f.at[pl.ds(1, groups - 1)], f_send).wait()


def per_device(
    in_plane_force, stiffness, stiffness_z, patch_dest, patch_pos, patch_flow, patch_conf
):
    groups = lax.axis_size("sec")
    _, layers, rows, columns = in_plane_force.shape
    inner_rows = rows // groups
    width = patch_flow.shape[-1]
    blocks = columns // width
    count = patch_pos.shape[2]
    depth = layers * groups
    cross = (
        stiffness_z.reshape(depth, inner_rows, blocks, width)
        .transpose(0, 2, 1, 3)
        .reshape(groups, layers * blocks * inner_rows, width)
    )
    f32, dma = jnp.float32, pltpu.SemaphoreType.DMA
    vmem = pltpu.VMEM
    out = pl.pallas_call(
        body,
        out_shape=pltpu.VMEM((2, groups, 8, width), f32),
        in_specs=[pl.BlockSpec(memory_space=pl.ANY)] * 7,
        out_specs=pl.BlockSpec(memory_space=pltpu.VMEM),
        scratch_shapes=[
            vmem((2, layers, rows + 2 * HALO, columns), f32),
            vmem((layers, rows + 2 * HALO, columns), f32),
            vmem((groups, 8, width), f32),
            vmem((1, count), jnp.int32),
            vmem((1, count), jnp.int32),
            vmem((2 * count, width), f32),
            vmem((count, width), f32),
            vmem((2, layers, rows, columns), f32),
            vmem((groups, 3, 8, width), f32),
            vmem((groups, 2, 8, width), f32),
            vmem((depth + 2, 8, width), f32),
            vmem((groups, 3, 8, width), f32),
            vmem((depth + 2, 8, width), f32),
            vmem((depth, 8, width), f32),
            vmem((depth, 8, width), f32),
            vmem((depth, 8, width), f32),
            dma((7,)),
            dma((2, 2)),
            dma((2, 2)),
            dma(()),
            dma(()),
            dma(()),
            dma(()),
            pltpu.SemaphoreType.REGULAR((2,)),
            pltpu.SemaphoreType.REGULAR,
        ],
        compiler_params=pltpu.CompilerParams(collective_id=0, has_side_effects=True),
        name="relax",
    )(
        in_plane_force,
        stiffness,
        cross,
        patch_dest.reshape(1, count),
        patch_pos.reshape(1, count),
        patch_flow.reshape(2 * count, width),
        patch_conf.reshape(count, width),
    )
    return (
        out.reshape(2, depth, blocks, inner_rows, width)
        .transpose(0, 1, 3, 2, 4)
        .reshape(2, depth, inner_rows, columns)
    )


def solution(mesh):
    placed = (
        P(None, "sec", "tile", None),
        P("sec", "tile", None),
        P(None, ("tile", "sec"), None),
        P("sec", "tile", None, None),
        P("sec", "tile", None),
        P("sec", "tile", None, None, None),
        P("sec", "tile", None, None),
    )
    return jax.shard_map(
        per_device,
        mesh=mesh,
        in_specs=placed,
        out_specs=P(None, None, ("tile", "sec"), None),
        check_vma=False,
    )
```
